32 devices in a mesh: groups: 2 (over y), cells: 8 (over z, x), freq: 2 (over core).
Axes of the slice: x: 2, y: 2, z: 4, core: 2. Of those that a mesh axis runs over, the one named last changes fastest.
Arguments:
- adjoint: float32 [2, 256], P(None, ('groups', 'cells')), parts along dimension 1, may hold values from -6 to 6
- target_x: float32 [256], P(('groups', 'cells')), parts along dimension 0, may hold values from 0 to 1024
- target_y: float32 [256], P(('groups', 'cells')), parts along dimension 0, may hold values from 0 to 8
- target_z: float32 [256], P(('groups', 'cells')), parts along dimension 0, may hold values from 256 to 512
- assignment: int32 [256], P(('groups', 'cells')), parts along dimension 0, may hold values from 0 to 63
- level_codes: int32 [16384], P(('groups', 'cells', 'freq')), parts along dimension 0, may hold values from 0 to 15
- cell_params: bfloat16 [8, 16384], P(None, ('groups', 'cells', 'freq')), parts along dimension 1, may hold values from -5 to 5
- level_table: bfloat16 [16, 256], replicated, may hold values from -4 to 4
- w_proj: bfloat16 [8, 256], replicated, may hold values from -2 to 2
- w_one: bfloat16 [256, 256], replicated, may hold values from -0.375 to 0.375
- b_one: float32 [256], replicated, may hold values from -3 to 3
- w_two: bfloat16 [256, 256], replicated, may hold values from -0.375 to 0.375
- b_two: float32 [256], replicated, may hold values from -3 to 3
- w_out: bfloat16 [256, 128], replicated, may hold values from -0.375 to 0.375
Outputs:
- grad_out: float32 [512, 128], P('groups'), parts along dimension 0
- grad_w2: float32 [512, 256], P('groups'), parts along dimension 0
- grad_b2: float32 [512], P('groups'), parts along dimension 0
- grad_w1: float32 [512, 256], P('groups'), parts along dimension 0
- grad_b1: float32 [512], P('groups'), parts along dimension 0
- grad_table: float32 [32, 256], P('groups'), parts along dimension 0
- grad_proj: float32 [16, 256], P('groups'), parts along dimension 0
- grad_params: float32 [8, 16384], P(None, ('groups', 'cells', 'freq')), parts along dimension 1
The draws below stay inside these ranges and needn't reach their ends.
There are 2 independent parts, one for each index of `groups`. The reference program is written for one: setup_inputs(seed, part) draws one part's arguments, and reference() takes and returns one part's arrays. A program takes and returns all parts, laid end to end along the dimension named above; an argument that names none is the same for every part. Nothing has to cross between parts.
All inputs are finite; a program needn't handle non-finite values.
Results may differ from the reference program's by a relative error of at most 0.01.
Values may be sent and summed in bfloat16 or wider, within the bound.
A program may use at most 64 MiB of HBM per device.

```python
import math
import jax
import jax.numpy as jnp
from jax import lax

F = 64
H = 256
LEVELS = 16
NP = 8
SIDE = 1024
CELLS = 8192
TARGETS = 128


def touch_ends(entries, key, smallest, largest):
    extent = entries.shape
    place = [jax.random.randint(jax.random.fold_in(key, axis), (), 0, extent[axis]) for axis in range(len(extent))]
    entries = entries.at[tuple(place)].set(smallest)
    longest = extent.index(max(extent))
    place[longest] = (place[longest] + 1) % extent[longest]
    return entries.at[tuple(place)].set(largest)


def block_levels(stream_key, dims, shards, low, high):
    def one(axis_at, parts):
        draws = jax.random.uniform(jax.random.fold_in(jax.random.fold_in(stream_key, 6), axis_at), (parts,), jnp.float32, low / len(shards), high / len(shards))
        return jnp.repeat(jnp.exp(draws), dims[axis_at] // parts).reshape((-1,) + (1,) * (len(dims) - axis_at - 1))

    factor_of = one(*shards[0])
    for cut in shards[1:]:
        factor_of = factor_of * one(*cut)
    return factor_of


def centred(key, extent, scale, most, pieces=(), kind=jnp.bfloat16):
    result = scale * jax.random.normal(key, extent, jnp.float32)
    if pieces:
        result = result * block_levels(key, extent, pieces, -0.22, 0.18)
    return jnp.clip(result, -most, most).astype(kind)


def setup_inputs(seed: int = 0, part: int = 0) -> dict:
    arg_keys = jax.random.split(jax.random.key(seed), 15)
    own_keys = jax.random.split(jax.random.fold_in(arg_keys[14], part), 15)
    adjoint = centred(own_keys[0], (2, TARGETS), 1.0, 6.0, ((1, 8),), jnp.float32)
    target_x = jnp.clip(1024.0 * jax.random.uniform(own_keys[1], (TARGETS,), jnp.float32) ** block_levels(own_keys[1], (TARGETS,), ((0, 8),), -0.2, 0.2), 0.0, 1024.0)
    target_y = jnp.clip(8.0 * jax.random.uniform(own_keys[2], (TARGETS,), jnp.float32) ** block_levels(own_keys[2], (TARGETS,), ((0, 8),), -0.2, 0.2), 0.0, 8.0)
    target_z = jnp.clip(256.0 + 256.0 * jax.random.uniform(own_keys[3], (TARGETS,), jnp.float32) ** block_levels(own_keys[3], (TARGETS,), ((0, 8),), -0.2, 0.2), 256.0, 512.0)
    assignment = touch_ends(jax.random.randint(own_keys[4], (TARGETS,), 0, F), jax.random.fold_in(own_keys[4], 1), 0, F - 1).astype(jnp.int32)
    level_codes = touch_ends(jax.random.randint(own_keys[5], (CELLS,), 0, LEVELS), jax.random.fold_in(own_keys[5], 1), 0, LEVELS - 1).astype(jnp.int32)
    cell_params = centred(own_keys[6], (NP, CELLS), 1.0, 5.0, ((1, 16),))
    level_table = centred(arg_keys[7], (LEVELS, H), 0.7, 4.0)
    w_proj = centred(arg_keys[8], (NP, H), NP ** -0.5, 2.0)
    w_one = centred(arg_keys[9], (H, H), H ** -0.5, 0.375)
    b_one = centred(arg_keys[10], (H,), 0.5, 3.0, (), jnp.float32)
    w_two = centred(arg_keys[11], (H, H), H ** -0.5, 0.375)
    b_two = centred(arg_keys[12], (H,), 0.5, 3.0, (), jnp.float32)
    w_out = centred(arg_keys[13], (H, 2 * F), H ** -0.5, 0.375)
    return dict(adjoint=adjoint, target_x=target_x, target_y=target_y, target_z=target_z, assignment=assignment, level_codes=level_codes, cell_params=cell_params, level_table=level_table, w_proj=w_proj, w_one=w_one, b_one=b_one, w_two=w_two, b_two=b_two, w_out=w_out)


wave_low = 1.0
wave_high = 3.0
kernel_gain = 150.0

def silu_slope(value):
    sigma = jax.nn.sigmoid(value)
    return sigma * (1.0 + value * (1.0 - sigma))

def contract(left, right, left_dim, right_dim):
    return lax.dot_general(left, right, (((left_dim,), (right_dim,)), ((), ())), preferred_element_type=jnp.float32)

def kernel_tile(point_x, point_y, point_z, freq_value, cell_col, cell_row, count_freq):
    wave = wave_low + (wave_high - wave_low) * freq_value / (count_freq - 1)
    offset_x = point_x[:, None] - cell_col[None, :]
    offset_y = point_y[:, None] - cell_row[None, :]
    square = offset_x * offset_x + offset_y * offset_y + (point_z * point_z)[:, None]
    distance = jnp.sqrt(square)
    amplitude = kernel_gain * point_z[:, None] / square
    phase = wave[:, None] * distance
    return ((amplitude * jnp.cos(phase)).astype(jnp.bfloat16), (amplitude * jnp.sin(phase)).astype(jnp.bfloat16))

def forward_pass(level_codes, cell_params, level_table, w_proj, w_one, b_one, w_two, b_two):
    levels = level_table.shape[0]
    onehot = (level_codes[:, None] == jnp.arange(levels, dtype=jnp.int32)[None, :]).astype(jnp.bfloat16)
    hidden_in = (jnp.dot(onehot, level_table, preferred_element_type=jnp.float32) + contract(cell_params, w_proj, 0, 0)).astype(jnp.bfloat16)
    pre_one = jnp.dot(hidden_in, w_one, preferred_element_type=jnp.float32) + b_one
    act_one = jax.nn.silu(pre_one).astype(jnp.bfloat16)
    pre_two = jnp.dot(act_one, w_two, preferred_element_type=jnp.float32) + b_two
    act_two = jax.nn.silu(pre_two).astype(jnp.bfloat16)
    return (onehot, hidden_in, pre_one, act_one, pre_two, act_two)

def upper_grads(spectra, w_out, act_one, pre_two, act_two):
    back_two = contract(spectra, w_out, 0, 1)
    delta_two = (back_two * silu_slope(pre_two)).astype(jnp.bfloat16)
    grad_out = contract(act_two, spectra, 0, 1)
    grad_w2 = contract(act_one, delta_two, 0, 0)
    grad_b2 = lax.optimization_barrier(jnp.sum(delta_two.astype(jnp.float32), axis=0))
    return ((grad_out, grad_w2, grad_b2), delta_two)

def lower_grads(delta_two, w_two, w_one, pre_one, hidden_in, onehot, cell_params, w_proj):
    back_one = contract(delta_two, w_two, 1, 1)
    delta_one = (back_one * silu_slope(pre_one)).astype(jnp.bfloat16)
    grad_w1 = contract(hidden_in, delta_one, 0, 0)
    grad_b1 = lax.optimization_barrier(jnp.sum(delta_one.astype(jnp.float32), axis=0))
    back_zero = contract(delta_one, w_one, 1, 1).astype(jnp.bfloat16)
    grad_table = contract(onehot, back_zero, 0, 0)
    grad_proj = contract(cell_params, back_zero, 1, 0)
    grad_params = contract(w_proj, back_zero, 1, 1)
    return ((grad_w1, grad_b1, grad_table, grad_proj), grad_params)

def reference(adjoint, target_x, target_y, target_z, assignment, level_codes, cell_params, level_table, w_proj, w_one, b_one, w_two, b_two, w_out):
    adj_round = lax.optimization_barrier(adjoint.astype(jnp.bfloat16)).astype(jnp.float32)
    freq_value = assignment.astype(jnp.float32)
    blocks = CELLS // SIDE
    scale = 1.0 / math.sqrt(CELLS)

    def step(carry, block):
        start = block * SIDE
        index = start + jnp.arange(SIDE, dtype=jnp.int32)
        cell_col = (index % SIDE).astype(jnp.float32)
        cell_row = (index // SIDE).astype(jnp.float32)
        kre, kim = kernel_tile(target_x, target_y, target_z, freq_value, cell_col, cell_row, F)
        kre, kim = lax.optimization_barrier((kre, kim))
        kre = kre.astype(jnp.float32)
        kim = kim.astype(jnp.float32)
        real_part = jax.ops.segment_sum(kre * adj_round[0][:, None] + kim * adj_round[1][:, None], assignment, num_segments=F)
        imag_part = jax.ops.segment_sum(kre * adj_round[1][:, None] - kim * adj_round[0][:, None], assignment, num_segments=F)
        spectra = jnp.concatenate([real_part, imag_part], axis=0).astype(jnp.bfloat16)
        codes_block = lax.dynamic_slice_in_dim(level_codes, start, SIDE)
        params_block = lax.dynamic_slice_in_dim(cell_params, start, SIDE, axis=1)
        onehot, hidden_in, pre_one, act_one, pre_two, act_two = forward_pass(codes_block, params_block, level_table, w_proj, w_one, b_one, w_two, b_two)
        upper, delta_two = upper_grads(spectra, w_out, act_one, pre_two, act_two)
        lower, grad_params = lower_grads(delta_two, w_two, w_one, pre_one, hidden_in, onehot, params_block, w_proj)
        carry = tuple((total + term for total, term in zip(carry, upper + lower)))
        return (carry, grad_params)
    init = (jnp.zeros((H, 2 * F), jnp.float32), jnp.zeros((H, H), jnp.float32), jnp.zeros((H,), jnp.float32), jnp.zeros((H, H), jnp.float32), jnp.zeros((H,), jnp.float32), jnp.zeros((LEVELS, H), jnp.float32), jnp.zeros((NP, H), jnp.float32))
    totals, params_grads = lax.scan(step, init, jnp.arange(blocks, dtype=jnp.int32))
    grad_params = jnp.moveaxis(params_grads, 0, 1).reshape(NP, CELLS)
    return (totals[0] * scale, totals[1] * scale, totals[2] * scale, totals[3] * scale, totals[4] * scale, totals[5] * scale, totals[6] * scale, grad_params)
```

```python
import functools
import math

import jax
import jax.numpy as jnp
from jax import lax
from jax.experimental import pallas as pl
from jax.experimental.pallas import tpu as pltpu
from jax.sharding import PartitionSpec as P

SIDE = 1024
LANES = 128
ROWS = 16
WIRE = jnp.bfloat16
VMEM_GRANT = 50331648

wave_low = 1.0
wave_high = 3.0
kernel_gain = 150.0

SINE = (4.44288292, -7.3082457, 3.60635441, -0.84611289, 0.10982699)
COSINE = (1.4142135, -6.97885099, 5.73946117, -1.88356299, 0.31069819)

f32 = jnp.float32
bf16 = jnp.bfloat16


def contract(left, right, left_dim, right_dim):
    return lax.dot_general(
        left, right, (((left_dim,), (right_dim,)), ((), ())), preferred_element_type=f32
    )


def horner(square, terms):
    total = terms[-1]
    for term in terms[-2::-1]:
        total = total * square + term
    return total


def each(low, high, step):
    if high - low <= 8:
        for k in range(low, high):
            step(k)
    else:

        @pl.loop(low, high)
        def _(k):
            step(k)


def silu_parts(pre):
    sig = 0.5 + 0.5 * jnp.tanh(0.5 * pre)
    act = pre * sig
    return act, sig + act * (1.0 - sig)


def split(value):
    high = value.astype(bf16)
    return high, (value - high.astype(f32)).astype(bf16)


def kernel(dims, *refs):
    inputs, results, loaded = refs[:14], refs[14:20], refs[20:34]
    (
        fin,
        fins,
        gc_ref,
        gw1_ref,
        gtp_ref,
        grow_ref,
    ) = results
    (
        gath,
        feat,
        column,
        w1t,
        w2t,
        tpt,
        bias,
        act1,
        slope1,
        act2,
        slope2,
        waves,
        left,
        spec,
        d2,
        d1,
        gc_mate,
        sbuf,
        ssml,
        rbuf,
        rsml,
        g_send,
        g_recv,
        f_send,
        f_recv,
        x_send,
        x_recv,
        o_send,
        o_recv,
        load_sem,
    ) = refs[34:]
    (
        adj_ref,
        x_ref,
        y_ref,
        z_ref,
        asg_ref,
        codes_ref,
        params_ref,
        table_ref,
        proj_ref,
        w1_ref,
        b1_ref,
        w2_ref,
        b2_ref,
        wo_ref,
    ) = loaded
    n, nf, per, rounds, scale = dims
    me = lax.axis_index("cells")
    core = lax.axis_index("freq")
    lead = nf - 1
    half = n // 2
    upper = me // half
    place = lax.rem(me, half)
    partner = lax.rem(me + half, n)
    cells = codes_ref.shape[1]
    local = x_ref.shape[1]
    targets = n * local
    hidden = w1_ref.shape[0]
    levels = table_ref.shape[0]
    n_par = proj_ref.shape[0]
    used = levels + n_par
    outs = wo_ref.shape[1]
    freqs = outs // 2
    width = per * local
    rows = feat.shape[1]
    chunks = fin.shape[0]
    top = hidden // 2

    def remote(src, dst, send, recv, device):
        return pltpu.make_async_remote_copy(
            src_ref=src,
            dst_ref=dst,
            send_sem=send,
            recv_sem=recv,
            device_id=device,
            device_id_type=pl.DeviceIdType.MESH,
        )

    def greet(device):
        pl.semaphore_signal(
            barrier, inc=1, device_id=device, device_id_type=pl.DeviceIdType.MESH
        )

    barrier = pltpu.get_barrier_semaphore()
    loads = [
        pltpu.make_async_copy(src, dst, load_sem.at[i])
        for i, (src, dst) in enumerate(zip(inputs, loaded))
    ]

    def get(*which):
        for i in which:
            loads[i].start()

    def have(*which):
        for i in which:
            loads[i].wait()

    def own_features():
        level = lax.broadcasted_iota(jnp.int32, (levels, cells), 0)
        line = lax.broadcasted_iota(jnp.int32, (rows - used, cells), 0)
        return jnp.concatenate(
            [
                jnp.where(codes_ref[...] == level, 1.0, 0.0),
                params_ref[...].astype(f32),
                jnp.where(line == 0, 1.0, 0.0),
            ],
            axis=0,
        ).astype(bf16)

    def base():
        return jnp.concatenate(
            [
                table_ref[...].astype(f32),
                proj_ref[...].astype(f32),
                jnp.zeros((rows - used, hidden), f32),
            ],
            axis=0,
        ).astype(bf16)

    def block_of(which, c):
        return which * nf + c

    mate = {"freq": nf - 1 - core}
    across = {"cells": partner, "freq": lead}

    def feat_mate():
        mine = feat.at[block_of(upper, core)]
        return remote(mine, mine, f_send.at[nf], f_recv.at[block_of(upper, core)], mate)

    def feat_across():
        mine = feat.at[block_of(upper, core)]
        return remote(mine, mine, f_send.at[core], f_recv.at[block_of(upper, core)], across)

    def rows_of(h):
        return pl.ds(h * top, top)

    def small_of(h):
        return pl.ds(h * (rows // 2), rows // 2)

    def piece(buffer, small, c, h):
        if c < chunks:
            return buffer.at[c, rows_of(h)]
        return small.at[small_of(h)]

    def give(c, h):
        view = piece(fin, fins, c, h)
        return remote(view, view, o_send.at[c, h], o_recv.at[c, h], mate)

    def give_params():
        return remote(gc_mate, gc_ref, o_send.at[chunks + 1, 0], o_recv.at[chunks + 1, 0], mate)

    order = [(c, h) for c in range(chunks + 1) for h in range(2)]

    def finish():
        total = fins[...]
        high, low = split(total)
        factors = jnp.concatenate([high, low], axis=0)
        basis = base()
        gw1_ref[...] = contract(jnp.concatenate([basis, basis], axis=0), factors, 0, 0)
        back = contract(factors, w1_ref[...], 1, 1)
        gtp_ref[...] = back[0:rows] + back[rows:]
        grow_ref[...] = total[used : used + 8]

    @pl.when(core != lead)
    def _():
        greet({"freq": lead})
        get(5, 6, 7, 8, 9)
        have(5, 6)
        feat[block_of(upper, core)] = own_features()
        pl.semaphore_wait(barrier, 2)
        feat_mate().start()
        feat_across().start()
        have(7, 8, 9)
        feat_mate().wait_send()
        feat_across().wait_send()
        for c, h in order:
            give(c, h).wait_recv()
        give_params().wait_recv()
        finish()

    @pl.when(core == lead)
    def _():
        def peer(k):
            return {"cells": lax.rem(me + k, n), "freq": lead}

        each(1, n, lambda k: greet(peer(k)))
        greet({"freq": 0})
        greet({"cells": partner, "freq": 0})
        get(*range(14))
        have(0, 1, 2, 3, 4)
        packet = jnp.concatenate(
            [
                adj_ref[...],
                x_ref[...],
                y_ref[...],
                z_ref[...],
                asg_ref[...].astype(f32),
                jnp.zeros((2, local), f32),
            ],
            axis=0,
        )
        spread = jnp.concatenate([packet] * per, axis=1)
        lane = lax.broadcasted_iota(jnp.int32, (8, width), 1)
        start = lax.rem(me, per) * local
        inside = jnp.logical_and(lane >= start, lane < start + local)
        gath[me] = jnp.where(inside, spread, 0.0)
        have(5, 6)
        feat[block_of(upper, lead)] = own_features()

        def packet_copy(k):
            return remote(gath.at[me], gath.at[me], g_send.at[k], g_recv.at[me], peer(k))

        def arrival(s):
            return remote(gath.at[s], gath.at[s], g_send.at[0], g_recv.at[s], peer(1))

        def feat_arrival(b):
            return remote(feat.at[b], feat.at[b], f_send.at[0], f_recv.at[b], peer(1))

        pl.semaphore_wait(barrier, n)
        each(1, n, lambda k: packet_copy(k).start())
        feat_across().start()

        have(7, 8, 9, 10, 11, 12, 13)
        w1t[...] = w1_ref[...].astype(f32).T.astype(bf16)
        w2t[...] = w2_ref[...].astype(f32).T.astype(bf16)
        tpt[...] = base().astype(f32).T.astype(bf16)
        bias[...] = jnp.concatenate(
            [b1_ref[...], b2_ref[...], jnp.zeros((6, hidden), f32)], axis=0
        ).T
        edge = lax.broadcasted_iota(jnp.int32, (ROWS, nf * 2 * cells), 0)
        act1[hidden : hidden + ROWS, :] = jnp.where(edge == 0, 1.0, 0.0).astype(bf16)

        def lanes_of(b):
            return pl.ds(pl.multiple_of(b * cells, cells), cells)

        def forward(b):
            here = lanes_of(b)
            hid = contract(tpt[...], feat[b], 1, 0).astype(bf16)
            act, slope = silu_parts(contract(w1t[...], hid, 1, 0) + bias[:, 0:1])
            act = act.astype(bf16)
            act1[0:hidden, here] = act
            slope1[:, here] = slope
            act, slope = silu_parts(contract(w2t[...], act, 1, 0) + bias[:, 1:2])
            act2[:, here] = act.astype(bf16)
            slope2[:, here] = slope

        def entries(s):
            column[...] = gath[s].T
            spot = column[pl.ds(pl.multiple_of(lax.rem(s, per) * local, local), local), :]
            px, py, pz, pf = spot[:, 2:3], spot[:, 3:4], spot[:, 4:5], spot[:, 5:6]
            turn = (wave_low + (wave_high - wave_low) * pf / (freqs - 1)) * (0.5 / math.pi)
            deep = pz * pz
            gain = kernel_gain * pz
            at_re = pl.ds(pl.multiple_of(s * local, local), local)
            at_im = pl.ds(pl.multiple_of(targets + s * local, local), local)
            for b in range(2 * nf):
                chip = place + (b // nf) * half
                first = (chip * nf + b % nf) * cells
                if SIDE % cells == 0:
                    row = (first // SIDE).astype(f32)
                    off = lax.rem(first, SIDE) + lax.broadcasted_iota(jnp.int32, (1, cells), 1)
                    col = off.astype(f32)
                else:
                    index = first + lax.broadcasted_iota(jnp.int32, (1, cells), 1)
                    col = (index % SIDE).astype(f32)
                    row = (index // SIDE).astype(f32)
                off_y = py - row
                off_x = px - col
                square = off_x * off_x + (off_y * off_y + deep)
                inverse = lax.rsqrt(square)
                distance = square * inverse
                distance = distance + (0.5 * inverse) * (square - distance * distance)
                phase = distance * turn
                rest = phase - jnp.floor(phase + 0.5)
                power = rest * rest
                sine = rest * horner(power, SINE)
                cosine = horner(power, COSINE)
                amplitude = (inverse * inverse) * gain
                scaled = amplitude * sine
                here = slice(b * cells, (b + 1) * cells)
                waves[at_re, here] = (amplitude - scaled * sine).astype(bf16)
                waves[at_im, here] = (scaled * cosine).astype(bf16)

        def section(s):
            @pl.when(s != me)
            def _():
                arrival(s).wait_recv()

            entries(s)

        forward(block_of(upper, lead))
        feat_arrival(block_of(upper, 0)).wait_recv()
        forward(block_of(upper, 0))

        @pl.loop(0, half)
        def _(i):
            section(upper * half + i)

        @pl.loop(0, nf)
        def _(c):
            b = block_of(1 - upper, c)
            feat_arrival(b).wait_recv()
            forward(b)

        @pl.loop(0, half)
        def _(i):
            section((1 - upper) * half + i)

        line = lax.broadcasted_iota(jnp.int32, (outs, width), 0)
        is_re = line < freqs
        freq_line = jnp.where(is_re, line, line - freqs).astype(f32)

        def weigh(group):
            block = gath[group * per]
            for j in range(1, per):
                block = block + gath[group * per + j]
            adj = block[0:2].astype(bf16).astype(f32)
            a0, a1 = adj[0:1], adj[1:2]
            chosen = freq_line == block[5:6]
            to = pl.multiple_of(group * width, width)
            left[:, pl.ds(to, width)] = jnp.where(
                chosen, jnp.where(is_re, a0, a1), 0.0
            ).astype(bf16)
            to = pl.multiple_of(targets + group * width, width)
            left[:, pl.ds(to, width)] = jnp.where(
                chosen, jnp.where(is_re, a1, -a0), 0.0
            ).astype(bf16)

        each(0, n // per, weigh)

        def swap(i, c, h):
            bit = (i + h * (rounds // 2)) % rounds
            side = lax.rem(me // (1 << bit), 2)
            other = me + (1 - 2 * side) * (1 << bit)
            return remote(
                piece(sbuf.at[i], ssml.at[i], c, h),
                piece(rbuf.at[i], rsml.at[i], c, h),
                x_send.at[i, c, h],
                x_recv.at[i, c, h],
                {"cells": other, "freq": lead},
            )

        spec[...] = contract(left[...], waves[...], 1, 0).astype(bf16)
        sbuf[0, 0] = contract(act2[...], spec[...], 1, 1).astype(WIRE)
        swap(0, 0, 0).start()
        swap(0, 0, 1).start()

        @pl.loop(0, 2 * nf)
        def _(b):
            here = lanes_of(b)
            back = contract(wo_ref[...], spec[:, here], 1, 0)
            d2[:, here] = (back * slope2[:, here]).astype(bf16)

        grad = contract(act1[...], d2[...], 1, 1)
        for c in range(1, chunks):
            sbuf[0, c] = grad[0:hidden, (c - 1) * outs : c * outs].astype(WIRE)
            for h in range(2):
                swap(0, c, h).start()
        grad_b2 = grad[hidden : hidden + 1]

        @pl.loop(0, 2 * nf)
        def _(b):
            here = lanes_of(b)
            back = contract(w2_ref[...], d2[:, here], 1, 0)
            d1[:, here] = (back * slope1[:, here]).astype(bf16)

        small = jnp.zeros((rows, hidden), f32)
        for b in range(2 * nf):
            small = small + contract(feat[b], d1[:, b * cells : (b + 1) * cells], 1, 1)
        line = lax.broadcasted_iota(jnp.int32, (rows, hidden), 0)
        ssml[0] = jnp.where(line == used + 1, grad_b2, small)
        for h in range(2):
            swap(0, chunks, h).start()

        high, low = split(contract(proj_ref[...], w1_ref[...], 1, 0))
        folded = jnp.concatenate([high.astype(f32), low.astype(f32)], axis=0).astype(bf16)
        own = pl.ds(pl.multiple_of(upper * (nf * cells), nf * cells), nf * cells)
        params = contract(folded, d1[:, own], 1, 0)
        params = params[0:n_par] + params[n_par:]
        gc_mate[...] = params[:, 0:cells]
        gc_ref[...] = params[:, cells:]
        give_params().start()

        for i in range(rounds):
            last = i == rounds - 1
            for c, h in order:
                swap(i, c, h).wait_recv()
                total = (
                    piece(sbuf.at[i], ssml.at[i], c, h)[...].astype(f32)
                    + piece(rbuf.at[i], rsml.at[i], c, h)[...].astype(f32)
                )
                if last:
                    target = piece(fin, fins, c, h)
                    target[...] = (total * scale).astype(target.dtype)
                    give(c, h).start()
                else:
                    target = piece(sbuf.at[i + 1], ssml.at[i + 1], c, h)
                    target[...] = total.astype(target.dtype)
                    swap(i + 1, c, h).start()
        finish()

        each(1, n, lambda k: packet_copy(k).wait_send())
        feat_across().wait_send()
        for i in range(rounds):
            for c, h in order:
                swap(i, c, h).wait_send()
        for c, h in order:
            give(c, h).wait_send()
        give_params().wait_send()


def unpack(
    fin,
    gc_in,
    gw1_in,
    gtp_in,
    grow_in,
    go_ref,
    gw2_ref,
    gb2_ref,
    gw1_ref,
    gb1_ref,
    gt_ref,
    gp_ref,
    gc_ref,
):
    outs = go_ref.shape[1]
    levels, n_par = gt_ref.shape[0], gp_ref.shape[0]
    go_ref[...] = fin[0].astype(f32)
    for c in range(1, fin.shape[0]):
        gw2_ref[:, (c - 1) * outs : c * outs] = fin[c].astype(f32)
    gw1_ref[...] = gw1_in[...]
    gb1_ref[...] = grow_in[0:1]
    gb2_ref[...] = grow_in[1:2]
    gt_ref[...] = gtp_in[0:levels]
    gp_ref[...] = gtp_in[levels : levels + n_par]
    gc_ref[...] = gc_in[...]


def round_up(value, step):
    return -(-value // step) * step


def body(
    adjoint,
    target_x,
    target_y,
    target_z,
    assignment,
    level_codes,
    cell_params,
    level_table,
    w_proj,
    w_one,
    b_one,
    w_two,
    b_two,
    w_out,
):
    n = lax.axis_size("cells")
    nf = lax.axis_size("freq")
    cells = level_codes.shape[0]
    local = target_x.shape[0]
    hidden = w_one.shape[0]
    levels = level_table.shape[0]
    n_par = w_proj.shape[0]
    outs = w_out.shape[1]
    per = math.gcd(n, max(1, LANES // local))
    half = n // 2
    rounds = half.bit_length() - 1
    assert nf == 2 and n == 2 << rounds
    rows = round_up(levels + n_par + 8, 2 * ROWS)
    chunks = 1 + hidden // outs
    blocks = 2 * nf
    every = blocks * cells
    targets = n * local
    scale = 1.0 / math.sqrt(cells * n * nf)
    vmem = pl.BlockSpec(memory_space=pltpu.VMEM)
    dma = pltpu.SemaphoreType.DMA
    args = (
        adjoint,
        target_x[None, :],
        target_y[None, :],
        target_z[None, :],
        assignment[None, :],
        level_codes[None, :],
        cell_params,
        level_table,
        w_proj,
        w_one,
        b_one[None, :],
        w_two,
        b_two[None, :],
        w_out,
    )
    packed = pl.pallas_call(
        functools.partial(kernel, (n, nf, per, rounds, scale)),
        out_shape=[
            pltpu.VMEM((chunks, hidden, outs), WIRE),
            pltpu.VMEM((rows, hidden), f32),
            pltpu.VMEM((n_par, cells), f32),
            pltpu.VMEM((hidden, hidden), f32),
            pltpu.VMEM((rows, hidden), f32),
            pltpu.VMEM((8, hidden), f32),
        ],
        in_specs=[pl.BlockSpec(memory_space=pltpu.HBM)] * 14,
        out_specs=[vmem] * 6,
        scratch_shapes=[pltpu.VMEM(arg.shape, arg.dtype) for arg in args]
        + [
            pltpu.VMEM((n, 8, per * local), f32),
            pltpu.VMEM((blocks, rows, cells), bf16),
            pltpu.VMEM((per * local, 8), f32),
            pltpu.VMEM((hidden, hidden), bf16),
            pltpu.VMEM((hidden, hidden), bf16),
            pltpu.VMEM((hidden, rows), bf16),
            pltpu.VMEM((hidden, 8), f32),
            pltpu.VMEM((hidden + ROWS, every), bf16),
            pltpu.VMEM((hidden, every), f32),
            pltpu.VMEM((hidden, every), bf16),
            pltpu.VMEM((hidden, every), f32),
            pltpu.VMEM((2 * targets, every), bf16),
            pltpu.VMEM((outs, 2 * targets), bf16),
            pltpu.VMEM((outs, every), bf16),
            pltpu.VMEM((hidden, every), bf16),
            pltpu.VMEM((hidden, every), bf16),
            pltpu.VMEM((n_par, cells), f32),
            pltpu.VMEM((rounds, chunks, hidden, outs), WIRE),
            pltpu.VMEM((rounds, rows, hidden), f32),
            pltpu.VMEM((rounds, chunks, hidden, outs), WIRE),
            pltpu.VMEM((rounds, rows, hidden), f32),
            dma((n,)),
            dma((n,)),
            dma((nf + 1,)),
            dma((blocks,)),
            dma((rounds, chunks + 1, 2)),
            dma((rounds, chunks + 1, 2)),
            dma((chunks + 2, 2)),
            dma((chunks + 2, 2)),
            dma((len(args),)),
        ],
        compiler_params=pltpu.CompilerParams(
            collective_id=0, has_side_effects=True, vmem_limit_bytes=VMEM_GRANT
        ),
        name="hologram_adjoint",
    )(*[pltpu.with_memory_space_constraint(arg, pltpu.HBM) for arg in args])
    fin, _, params, g_one, g_low, g_rows = packed
    results = pl.pallas_call(
        unpack,
        out_shape=[
            jax.ShapeDtypeStruct((hidden, outs), f32),
            jax.ShapeDtypeStruct((hidden, hidden), f32),
            jax.ShapeDtypeStruct((1, hidden), f32),
            jax.ShapeDtypeStruct((hidden, hidden), f32),
            jax.ShapeDtypeStruct((1, hidden), f32),
            jax.ShapeDtypeStruct((levels, hidden), f32),
            jax.ShapeDtypeStruct((n_par, hidden), f32),
            jax.ShapeDtypeStruct((n_par, cells), f32),
        ],
        in_specs=[vmem] * 5,
        out_specs=[vmem] * 8,
        compiler_params=pltpu.CompilerParams(vmem_limit_bytes=VMEM_GRANT // 4),
        name="unpack",
    )(fin, params, g_one, g_low, g_rows)
    grad_out, grad_w2, grad_b2, grad_w1, grad_b1, grad_table, grad_proj, grad_params = results
    return (
        grad_out,
        grad_w2,
        grad_b2[0],
        grad_w1,
        grad_b1[0],
        grad_table,
        grad_proj,
        grad_params,
    )


def solution(mesh):
    split_all = ("groups", "cells", "freq")
    points = ("groups", "cells")
    placed = (
        P(None, points),
        P(points),
        P(points),
        P(points),
        P(points),
        P(split_all),
        P(None, split_all),
    ) + (P(),) * 7
    return jax.shard_map(
        body,
        mesh=mesh,
        in_specs=placed,
        out_specs=(
            P("groups", None),
            P("groups", None),
            P("groups"),
            P("groups", None),
            P("groups"),
            P("groups", None),
            P("groups", None),
            P(None, split_all),
        ),
        check_vma=False,
    )
```

```python
import functools
import math

import jax
import jax.numpy as jnp
from jax import lax
from jax.experimental import pallas as pl
from jax.experimental.pallas import tpu as pltpu
from jax.sharding import PartitionSpec as P

SIDE = 1024
LANES = 128
ROWS = 16
WIRE = jnp.bfloat16
VMEM_GRANT = 50331648

wave_low = 1.0
wave_high = 3.0
kernel_gain = 150.0

SINE = (4.44288292, -7.3082457, 3.60635441, -0.84611289, 0.10982699)
COSINE = (1.4142135, -6.97885099, 5.73946117, -1.88356299, 0.31069819)

f32 = jnp.float32
bf16 = jnp.bfloat16


def contract(left, right, left_dim, right_dim):
    return lax.dot_general(
        left, right, (((left_dim,), (right_dim,)), ((), ())), preferred_element_type=f32
    )


def horner(square, terms):
    total = terms[-1]
    for term in terms[-2::-1]:
        total = total * square + term
    return total


def each(low, high, step):
    if high - low <= 8:
        for k in range(low, high):
            step(k)
    else:

        @pl.loop(low, high)
        def _(k):
            step(k)


def silu_parts(pre):
    sig = 0.5 + 0.5 * jnp.tanh(0.5 * pre)
    act = pre * sig
    return act, sig + act * (1.0 - sig)


def split(value):
    high = value.astype(bf16)
    return high, (value - high.astype(f32)).astype(bf16)


def kernel(dims, *refs):
    inputs, results, loaded = refs[:14], refs[14:20], refs[20:34]
    (
        fin,
        fins,
        gc_ref,
        gw1_ref,
        gtp_ref,
        grow_ref,
    ) = results
    (
        gath,
        feat,
        column,
        w1t,
        w2t,
        tpt,
        bias,
        act1,
        slope1,
        act2,
        slope2,
        waves,
        left,
        spec,
        d2,
        d1,
        gc_mate,
        sbuf,
        ssml,
        rbuf,
        rsml,
        g_send,
        g_recv,
        f_send,
        f_recv,
        x_send,
        x_recv,
        o_send,
        o_recv,
        load_sem,
    ) = refs[34:]
    (
        adj_ref,
        x_ref,
        y_ref,
        z_ref,
        asg_ref,
        codes_ref,
        params_ref,
        table_ref,
        proj_ref,
        w1_ref,
        b1_ref,
        w2_ref,
        b2_ref,
        wo_ref,
    ) = loaded
    n, nf, per, rounds, scale = dims
    me = lax.axis_index("cells")
    core = lax.axis_index("freq")
    lead = nf - 1
    half = n // 2
    upper = me // half
    place = lax.rem(me, half)
    partner = lax.rem(me + half, n)
    cells = codes_ref.shape[1]
    local = x_ref.shape[1]
    targets = n * local
    hidden = w1_ref.shape[0]
    levels = table_ref.shape[0]
    n_par = proj_ref.shape[0]
    used = levels + n_par
    outs = wo_ref.shape[1]
    freqs = outs // 2
    width = per * local
    rows = feat.shape[1]
    chunks = fin.shape[0]
    top = hidden // 2

    def remote(src, dst, send, recv, device):
        return pltpu.make_async_remote_copy(
            src_ref=src,
            dst_ref=dst,
            send_sem=send,
            recv_sem=recv,
            device_id=device,
            device_id_type=pl.DeviceIdType.MESH,
        )

    def greet(device):
        pl.semaphore_signal(
            barrier, inc=1, device_id=device, device_id_type=pl.DeviceIdType.MESH
        )

    barrier = pltpu.get_barrier_semaphore()
    loads = [
        pltpu.make_async_copy(src, dst, load_sem.at[i])
        for i, (src, dst) in enumerate(zip(inputs, loaded))
    ]

    def get(*which):
        for i in which:
            loads[i].start()

    def have(*which):
        for i in which:
            loads[i].wait()

    def own_features():
        level = lax.broadcasted_iota(jnp.int32, (levels, cells), 0)
        line = lax.broadcasted_iota(jnp.int32, (rows - used, cells), 0)
        return jnp.concatenate(
            [
                jnp.where(codes_ref[...] == level, 1.0, 0.0),
                params_ref[...].astype(f32),
                jnp.where(line == 0, 1.0, 0.0),
            ],
            axis=0,
        ).astype(bf16)

    def base():
        return jnp.concatenate(
            [
                table_ref[...].astype(f32),
                proj_ref[...].astype(f32),
                jnp.zeros((rows - used, hidden), f32),
            ],
            axis=0,
        ).astype(bf16)

    def block_of(which, c):
        return which * nf + c

    mate = {"freq": nf - 1 - core}
    across = {"cells": partner, "freq": lead}

    def feat_mate():
        mine = feat.at[block_of(upper, core)]
        return remote(mine, mine, f_send.at[nf], f_recv.at[block_of(upper, core)], mate)

    def feat_across():
        mine = feat.at[block_of(upper, core)]
        return remote(mine, mine, f_send.at[core], f_recv.at[block_of(upper, core)], across)

    def rows_of(h):
        return pl.ds(h * top, top)

    def small_of(h):
        return pl.ds(h * (rows // 2), rows // 2)

    def piece(buffer, small, c, h):
        if c < chunks:
            return buffer.at[c, rows_of(h)]
        return small.at[small_of(h)]

    def give(c, h):
        view = piece(fin, fins, c, h)
        return remote(view, view, o_send.at[c, h], o_recv.at[c, h], mate)

    def give_params():
        return remote(gc_mate, gc_ref, o_send.at[chunks + 1, 0], o_recv.at[chunks + 1, 0], mate)

    order = [(c, h) for c in range(chunks + 1) for h in range(2)]

    def finish():
        total = fins[...]
        high, low = split(total)
        factors = jnp.concatenate([high, low], axis=0)
        basis = base()
        gw1_ref[...] = contract(jnp.concatenate([basis, basis], axis=0), factors, 0, 0)
        back = contract(factors, w1_ref[...], 1, 1)
        gtp_ref[...] = back[0:rows] + back[rows:]
        grow_ref[...] = total[used : used + 8]

    @pl.when(core != lead)
    def _():
        greet({"freq": lead})
        get(5, 6, 7, 8, 9)
        have(5, 6)
        feat[block_of(upper, core)] = own_features()
        pl.semaphore_wait(barrier, 2)
        feat_mate().start()
        feat_across().start()
        have(7, 8, 9)
        feat_mate().wait_send()
        feat_across().wait_send()
        for c, h in order:
            give(c, h).wait_recv()
        give_params().wait_recv()
        finish()

    @pl.when(core == lead)
    def _():
        def peer(k):
            return {"cells": lax.rem(me + k, n), "freq": lead}

        each(1, n, lambda k: greet(peer(k)))
        greet({"freq": 0})
        greet({"cells": partner, "freq": 0})
        get(*range(14))
        have(0, 1, 2, 3, 4)
        packet = jnp.concatenate(
            [
                adj_ref[...],
                x_ref[...],
                y_ref[...],
                z_ref[...],
                asg_ref[...].astype(f32),
                jnp.zeros((2, local), f32),
            ],
            axis=0,
        )
        spread = jnp.concatenate([packet] * per, axis=1)
        lane = lax.broadcasted_iota(jnp.int32, (8, width), 1)
        start = lax.rem(me, per) * local
        inside = jnp.logical_and(lane >= start, lane < start + local)
        gath[me] = jnp.where(inside, spread, 0.0)
        have(5, 6)
        feat[block_of(upper, lead)] = own_features()

        def packet_copy(k):
            return remote(gath.at[me], gath.at[me], g_send.at[k], g_recv.at[me], peer(k))

        def arrival(s):
            return remote(gath.at[s], gath.at[s], g_send.at[0], g_recv.at[s], peer(1))

        def feat_arrival(b):
            return remote(feat.at[b], feat.at[b], f_send.at[0], f_recv.at[b], peer(1))

        pl.semaphore_wait(barrier, n)
        each(1, n, lambda k: packet_copy(k).start())
        feat_across().start()

        have(7, 8, 9, 10, 11, 12, 13)
        w1t[...] = w1_ref[...].astype(f32).T.astype(bf16)
        w2t[...] = w2_ref[...].astype(f32).T.astype(bf16)
        tpt[...] = base().astype(f32).T.astype(bf16)
        bias[...] = jnp.concatenate(
            [b1_ref[...], b2_ref[...], jnp.zeros((6, hidden), f32)], axis=0
        ).T
        edge = lax.broadcasted_iota(jnp.int32, (ROWS, nf * 2 * cells), 0)
        act1[hidden : hidden + ROWS, :] = jnp.where(edge == 0, 1.0, 0.0).astype(bf16)

        def features(which):
            return jnp.concatenate([feat[block_of(which, c)] for c in range(nf)], axis=1)

        def forward(which):
            here = pl.ds(pl.multiple_of(which * nf * cells, nf * cells), nf * cells)
            hid = contract(tpt[...], features(which), 1, 0).astype(bf16)
            act, slope = silu_parts(contract(w1t[...], hid, 1, 0) + bias[:, 0:1])
            act = act.astype(bf16)
            act1[0:hidden, here] = act
            slope1[:, here] = slope
            act, slope = silu_parts(contract(w2t[...], act, 1, 0) + bias[:, 1:2])
            act2[:, here] = act.astype(bf16)
            slope2[:, here] = slope

        def entries(s, slot):
            column[slot] = gath[s].T
            spot = column[slot, pl.ds(pl.multiple_of(lax.rem(s, per) * local, local), local), :]
            px, py, pz, pf = spot[:, 2:3], spot[:, 3:4], spot[:, 4:5], spot[:, 5:6]
            turn = (wave_low + (wave_high - wave_low) * pf / (freqs - 1)) * (0.5 / math.pi)
            deep = pz * pz
            gain = kernel_gain * pz
            at_re = pl.ds(pl.multiple_of(s * local, local), local)
            at_im = pl.ds(pl.multiple_of(targets + s * local, local), local)
            for b in range(2 * nf):
                chip = place + (b // nf) * half
                first = (chip * nf + b % nf) * cells
                if SIDE % cells == 0:
                    row = (first // SIDE).astype(f32)
                    off = lax.rem(first, SIDE) + lax.broadcasted_iota(jnp.int32, (1, cells), 1)
                    col = off.astype(f32)
                else:
                    index = first + lax.broadcasted_iota(jnp.int32, (1, cells), 1)
                    col = (index % SIDE).astype(f32)
                    row = (index // SIDE).astype(f32)
                off_y = py - row
                off_x = px - col
                square = off_x * off_x + (off_y * off_y + deep)
                inverse = lax.rsqrt(square)
                distance = square * inverse
                distance = distance + (0.5 * inverse) * (square - distance * distance)
                phase = distance * turn
                rest = phase - jnp.floor(phase + 0.5)
                power = rest * rest
                sine = rest * horner(power, SINE)
                cosine = horner(power, COSINE)
                amplitude = (inverse * inverse) * gain
                scaled = amplitude * sine
                here = slice(b * cells, (b + 1) * cells)
                waves[at_re, here] = (amplitude - scaled * sine).astype(bf16)
                waves[at_im, here] = (scaled * cosine).astype(bf16)

        def section(first):
            @pl.loop(0, half // 2)
            def _(i):
                pair = (first + 2 * i, first + 2 * i + 1)
                for s in pair:

                    @pl.when(s != me)
                    def _():
                        arrival(s).wait_recv()

                for slot, s in enumerate(pair):
                    entries(s, slot)

        feat_arrival(block_of(upper, 0)).wait_recv()
        forward(upper)
        section(upper * half)
        for c in range(nf):
            feat_arrival(block_of(1 - upper, c)).wait_recv()
        forward(1 - upper)
        section((1 - upper) * half)

        line = lax.broadcasted_iota(jnp.int32, (outs, width), 0)
        is_re = line < freqs
        freq_line = jnp.where(is_re, line, line - freqs).astype(f32)

        def weigh(group):
            block = gath[group * per]
            for j in range(1, per):
                block = block + gath[group * per + j]
            adj = block[0:2].astype(bf16).astype(f32)
            a0, a1 = adj[0:1], adj[1:2]
            chosen = freq_line == block[5:6]
            to = pl.multiple_of(group * width, width)
            left[:, pl.ds(to, width)] = jnp.where(
                chosen, jnp.where(is_re, a0, a1), 0.0
            ).astype(bf16)
            to = pl.multiple_of(targets + group * width, width)
            left[:, pl.ds(to, width)] = jnp.where(
                chosen, jnp.where(is_re, a1, -a0), 0.0
            ).astype(bf16)

        each(0, n // per, weigh)

        def swap(i, c, h):
            bit = (i + h * (rounds // 2)) % rounds
            side = lax.rem(me // (1 << bit), 2)
            other = me + (1 - 2 * side) * (1 << bit)
            return remote(
                piece(sbuf.at[i], ssml.at[i], c, h),
                piece(rbuf.at[i], rsml.at[i], c, h),
                x_send.at[i, c, h],
                x_recv.at[i, c, h],
                {"cells": other, "freq": lead},
            )

        spec[...] = contract(left[...], waves[...], 1, 0).astype(bf16)
        sbuf[0, 0] = contract(act2[...], spec[...], 1, 1).astype(WIRE)
        swap(0, 0, 0).start()
        swap(0, 0, 1).start()

        back = contract(wo_ref[...], spec[...], 1, 0)
        d2[...] = (back * slope2[...]).astype(bf16)

        grad = contract(act1[...], d2[...], 1, 1)
        for c in range(1, chunks):
            sbuf[0, c] = grad[0:hidden, (c - 1) * outs : c * outs].astype(WIRE)
            for h in range(2):
                swap(0, c, h).start()
        grad_b2 = grad[hidden : hidden + 1]

        back = contract(w2_ref[...], d2[...], 1, 0)
        d1[...] = (back * slope1[...]).astype(bf16)
        both = jnp.concatenate([features(which) for which in range(2)], axis=1)
        small = contract(both, d1[...], 1, 1)
        line = lax.broadcasted_iota(jnp.int32, (rows, hidden), 0)
        ssml[0] = jnp.where(line == used + 1, grad_b2, small)
        for h in range(2):
            swap(0, chunks, h).start()

        high, low = split(contract(proj_ref[...], w1_ref[...], 1, 0))
        folded = jnp.concatenate([high.astype(f32), low.astype(f32)], axis=0).astype(bf16)
        own = pl.ds(pl.multiple_of(upper * (nf * cells), nf * cells), nf * cells)
        params = contract(folded, d1[:, own], 1, 0)
        params = params[0:n_par] + params[n_par:]
        gc_mate[...] = params[:, 0:cells]
        gc_ref[...] = params[:, cells:]
        give_params().start()

        for i in range(rounds):
            last = i == rounds - 1
            for c, h in order:
                swap(i, c, h).wait_recv()
                total = (
                    piece(sbuf.at[i], ssml.at[i], c, h)[...].astype(f32)
                    + piece(rbuf.at[i], rsml.at[i], c, h)[...].astype(f32)
                )
                if last:
                    target = piece(fin, fins, c, h)
                    target[...] = (total * scale).astype(target.dtype)
                    give(c, h).start()
                else:
                    target = piece(sbuf.at[i + 1], ssml.at[i + 1], c, h)
                    target[...] = total.astype(target.dtype)
                    swap(i + 1, c, h).start()
        finish()

        each(1, n, lambda k: packet_copy(k).wait_send())
        feat_across().wait_send()
        for i in range(rounds):
            for c, h in order:
                swap(i, c, h).wait_send()
        for c, h in order:
            give(c, h).wait_send()
        give_params().wait_send()


def unpack(
    fin,
    gc_in,
    gw1_in,
    gtp_in,
    grow_in,
    go_ref,
    gw2_ref,
    gb2_ref,
    gw1_ref,
    gb1_ref,
    gt_ref,
    gp_ref,
    gc_ref,
):
    outs = go_ref.shape[1]
    levels, n_par = gt_ref.shape[0], gp_ref.shape[0]
    go_ref[...] = fin[0].astype(f32)
    for c in range(1, fin.shape[0]):
        gw2_ref[:, (c - 1) * outs : c * outs] = fin[c].astype(f32)
    gw1_ref[...] = gw1_in[...]
    gb1_ref[...] = grow_in[0:1]
    gb2_ref[...] = grow_in[1:2]
    gt_ref[...] = gtp_in[0:levels]
    gp_ref[...] = gtp_in[levels : levels + n_par]
    gc_ref[...] = gc_in[...]


def round_up(value, step):
    return -(-value // step) * step


def body(
    adjoint,
    target_x,
    target_y,
    target_z,
    assignment,
    level_codes,
    cell_params,
    level_table,
    w_proj,
    w_one,
    b_one,
    w_two,
    b_two,
    w_out,
):
    n = lax.axis_size("cells")
    nf = lax.axis_size("freq")
    cells = level_codes.shape[0]
    local = target_x.shape[0]
    hidden = w_one.shape[0]
    levels = level_table.shape[0]
    n_par = w_proj.shape[0]
    outs = w_out.shape[1]
    per = math.gcd(n, max(1, LANES // local))
    half = n // 2
    rounds = half.bit_length() - 1
    assert nf == 2 and n == 2 << rounds
    rows = round_up(levels + n_par + 8, 2 * ROWS)
    chunks = 1 + hidden // outs
    blocks = 2 * nf
    every = blocks * cells
    targets = n * local
    scale = 1.0 / math.sqrt(cells * n * nf)
    vmem = pl.BlockSpec(memory_space=pltpu.VMEM)
    dma = pltpu.SemaphoreType.DMA
    args = (
        adjoint,
        target_x[None, :],
        target_y[None, :],
        target_z[None, :],
        assignment[None, :],
        level_codes[None, :],
        cell_params,
        level_table,
        w_proj,
        w_one,
        b_one[None, :],
        w_two,
        b_two[None, :],
        w_out,
    )
    packed = pl.pallas_call(
        functools.partial(kernel, (n, nf, per, rounds, scale)),
        out_shape=[
            pltpu.VMEM((chunks, hidden, outs), WIRE),
            pltpu.VMEM((rows, hidden), f32),
            pltpu.VMEM((n_par, cells), f32),
            pltpu.VMEM((hidden, hidden), f32),
            pltpu.VMEM((rows, hidden), f32),
            pltpu.VMEM((8, hidden), f32),
        ],
        in_specs=[pl.BlockSpec(memory_space=pltpu.HBM)] * 14,
        out_specs=[vmem] * 6,
        scratch_shapes=[pltpu.VMEM(arg.shape, arg.dtype) for arg in args]
        + [
            pltpu.VMEM((n, 8, per * local), f32),
            pltpu.VMEM((blocks, rows, cells), bf16),
            pltpu.VMEM((2, per * local, 8), f32),
            pltpu.VMEM((hidden, hidden), bf16),
            pltpu.VMEM((hidden, hidden), bf16),
            pltpu.VMEM((hidden, rows), bf16),
            pltpu.VMEM((hidden, 8), f32),
            pltpu.VMEM((hidden + ROWS, every), bf16),
            pltpu.VMEM((hidden, every), f32),
            pltpu.VMEM((hidden, every), bf16),
            pltpu.VMEM((hidden, every), f32),
            pltpu.VMEM((2 * targets, every), bf16),
            pltpu.VMEM((outs, 2 * targets), bf16),
            pltpu.VMEM((outs, every), bf16),
            pltpu.VMEM((hidden, every), bf16),
            pltpu.VMEM((hidden, every), bf16),
            pltpu.VMEM((n_par, cells), f32),
            pltpu.VMEM((rounds, chunks, hidden, outs), WIRE),
            pltpu.VMEM((rounds, rows, hidden), f32),
            pltpu.VMEM((rounds, chunks, hidden, outs), WIRE),
            pltpu.VMEM((rounds, rows, hidden), f32),
            dma((n,)),
            dma((n,)),
            dma((nf + 1,)),
            dma((blocks,)),
            dma((rounds, chunks + 1, 2)),
            dma((rounds, chunks + 1, 2)),
            dma((chunks + 2, 2)),
            dma((chunks + 2, 2)),
            dma((len(args),)),
        ],
        compiler_params=pltpu.CompilerParams(
            collective_id=0, has_side_effects=True, vmem_limit_bytes=VMEM_GRANT
        ),
        name="hologram_adjoint",
    )(*[pltpu.with_memory_space_constraint(arg, pltpu.HBM) for arg in args])
    fin, _, params, g_one, g_low, g_rows = packed
    results = pl.pallas_call(
        unpack,
        out_shape=[
            jax.ShapeDtypeStruct((hidden, outs), f32),
            jax.ShapeDtypeStruct((hidden, hidden), f32),
            jax.ShapeDtypeStruct((1, hidden), f32),
            jax.ShapeDtypeStruct((hidden, hidden), f32),
            jax.ShapeDtypeStruct((1, hidden), f32),
            jax.ShapeDtypeStruct((levels, hidden), f32),
            jax.ShapeDtypeStruct((n_par, hidden), f32),
            jax.ShapeDtypeStruct((n_par, cells), f32),
        ],
        in_specs=[vmem] * 5,
        out_specs=[vmem] * 8,
        compiler_params=pltpu.CompilerParams(vmem_limit_bytes=VMEM_GRANT // 4),
        name="unpack",
    )(fin, params, g_one, g_low, g_rows)
    grad_out, grad_w2, grad_b2, grad_w1, grad_b1, grad_table, grad_proj, grad_params = results
    return (
        grad_out,
        grad_w2,
        grad_b2[0],
        grad_w1,
        grad_b1[0],
        grad_table,
        grad_proj,
        grad_params,
    )


def solution(mesh):
    split_all = ("groups", "cells", "freq")
    points = ("groups", "cells")
    placed = (
        P(None, points),
        P(points),
        P(points),
        P(points),
        P(points),
        P(split_all),
        P(None, split_all),
    ) + (P(),) * 7
    return jax.shard_map(
        body,
        mesh=mesh,
        in_specs=placed,
        out_specs=(
            P("groups", None),
            P("groups", None),
            P("groups"),
            P("groups", None),
            P("groups"),
            P("groups", None),
            P("groups", None),
            P(None, split_all),
        ),
        check_vma=False,
    )
```

```python
import functools
import math

import jax
import jax.numpy as jnp
from jax import lax
from jax.experimental import pallas as pl
from jax.experimental.pallas import tpu as pltpu
from jax.sharding import PartitionSpec as P

SIDE = 1024
LANES = 128
ROWS = 16
WIRE = jnp.bfloat16
VMEM_GRANT = 50331648

wave_low = 1.0
wave_high = 3.0
kernel_gain = 150.0

SINE = (4.44288292, -7.3082457, 3.60635441, -0.84611289, 0.10982699)
COSINE = (1.4142135, -6.97885099, 5.73946117, -1.88356299, 0.31069819)

f32 = jnp.float32
bf16 = jnp.bfloat16


def contract(left, right, left_dim, right_dim):
    return lax.dot_general(
        left, right, (((left_dim,), (right_dim,)), ((), ())), preferred_element_type=f32
    )


def horner(square, terms):
    total = terms[-1]
    for term in terms[-2::-1]:
        total = total * square + term
    return total


def each(low, high, step):
    if high - low <= 8:
        for k in range(low, high):
            step(k)
    else:

        @pl.loop(low, high)
        def _(k):
            step(k)


def silu_parts(pre):
    sig = 0.5 + 0.5 * jnp.tanh(0.5 * pre)
    act = pre * sig
    return act, sig + act * (1.0 - sig)


def split(value):
    high = value.astype(bf16)
    return high, (value - high.astype(f32)).astype(bf16)


def kernel(dims, *refs):
    inputs, results, loaded = refs[:14], refs[14:20], refs[20:34]
    (
        fin,
        fins,
        gc_ref,
        gw1_ref,
        gtp_ref,
        grow_ref,
    ) = results
    (
        gath,
        codes_all,
        pars_all,
        feat,
        column,
        w1t,
        w2t,
        tpt,
        bias,
        act1,
        slope1,
        act2,
        slope2,
        waves,
        left,
        spec,
        d2,
        d1,
        gc_mate,
        sbuf,
        ssml,
        rbuf,
        rsml,
        g_send,
        g_recv,
        f_send,
        f_recv,
        x_send,
        x_recv,
        o_send,
        o_recv,
        load_sem,
    ) = refs[34:]
    (
        adj_ref,
        x_ref,
        y_ref,
        z_ref,
        asg_ref,
        codes_ref,
        params_ref,
        table_ref,
        proj_ref,
        w1_ref,
        b1_ref,
        w2_ref,
        b2_ref,
        wo_ref,
    ) = loaded
    n, nf, per, rounds, scale = dims
    me = lax.axis_index("cells")
    core = lax.axis_index("freq")
    lead = nf - 1
    half = n // 2
    upper = me // half
    place = lax.rem(me, half)
    partner = lax.rem(me + half, n)
    cells = codes_ref.shape[1]
    local = x_ref.shape[1]
    targets = n * local
    hidden = w1_ref.shape[0]
    levels = table_ref.shape[0]
    n_par = proj_ref.shape[0]
    used = levels + n_par
    outs = wo_ref.shape[1]
    freqs = outs // 2
    width = per * local
    rows = feat.shape[1]
    chunks = fin.shape[0]
    top = hidden // 2

    def remote(src, dst, send, recv, device):
        return pltpu.make_async_remote_copy(
            src_ref=src,
            dst_ref=dst,
            send_sem=send,
            recv_sem=recv,
            device_id=device,
            device_id_type=pl.DeviceIdType.MESH,
        )

    def greet(device):
        pl.semaphore_signal(
            barrier, inc=1, device_id=device, device_id_type=pl.DeviceIdType.MESH
        )

    barrier = pltpu.get_barrier_semaphore()
    loads = [
        pltpu.make_async_copy(src, dst, load_sem.at[i])
        for i, (src, dst) in enumerate(zip(inputs, loaded))
    ]

    def get(*which):
        for i in which:
            loads[i].start()

    def have(*which):
        for i in which:
            loads[i].wait()

    def own_cells():
        mine = block_of(upper, core)
        codes_all[mine] = codes_ref[...]
        wide = params_ref[...].astype(f32)
        pars_all[mine] = jnp.concatenate(
            [wide[:, : cells // 2], wide[:, cells // 2 :]], axis=0
        ).astype(bf16)

    def make_features(b):
        level = lax.broadcasted_iota(jnp.int32, (levels, cells), 0)
        line = lax.broadcasted_iota(jnp.int32, (rows - used, cells), 0)
        stacked = pars_all[b].astype(f32)
        feat[b] = jnp.concatenate(
            [
                jnp.where(codes_all[b] == level, 1.0, 0.0),
                jnp.concatenate([stacked[0:n_par], stacked[n_par:]], axis=1),
                jnp.where(line == 0, 1.0, 0.0),
            ],
            axis=0,
        ).astype(bf16)

    def base():
        return jnp.concatenate(
            [
                table_ref[...].astype(f32),
                proj_ref[...].astype(f32),
                jnp.zeros((rows - used, hidden), f32),
            ],
            axis=0,
        ).astype(bf16)

    def block_of(which, c):
        return which * nf + c

    mate = {"freq": nf - 1 - core}
    across = {"cells": partner, "freq": lead}

    def cell_copies(c, device):
        mine = block_of(upper, c)
        return [
            remote(part.at[mine], part.at[mine], f_send.at[c, i], f_recv.at[mine, i], device)
            for i, part in enumerate((codes_all, pars_all))
        ]

    def near(k, c):
        return {"cells": upper * half + lax.rem(place + k, half), "freq": c}

    def far(k, c):
        return {"cells": (1 - upper) * half + lax.rem(place + k, half), "freq": c}

    def packet_copy(k, device):
        return remote(gath.at[me], gath.at[me], g_send.at[k], g_recv.at[me], device)

    def own_packet():
        packet = jnp.concatenate(
            [
                adj_ref[...],
                x_ref[...],
                y_ref[...],
                z_ref[...],
                asg_ref[...].astype(f32),
                jnp.zeros((2, local), f32),
            ],
            axis=0,
        )
        spread = jnp.concatenate([packet] * per, axis=1)
        lane = lax.broadcasted_iota(jnp.int32, (8, width), 1)
        start = lax.rem(me, per) * local
        inside = jnp.logical_and(lane >= start, lane < start + local)
        gath[me] = jnp.where(inside, spread, 0.0)

    def rows_of(h):
        return pl.ds(h * top, top)

    def small_of(h):
        return pl.ds(h * (rows // 2), rows // 2)

    def piece(buffer, small, c, h):
        if c < chunks:
            return buffer.at[c, rows_of(h)]
        return small.at[small_of(h)]

    def give(c, h):
        view = piece(fin, fins, c, h)
        return remote(view, view, o_send.at[c, h], o_recv.at[c, h], mate)

    def give_params():
        return remote(gc_mate, gc_ref, o_send.at[chunks + 1, 0], o_recv.at[chunks + 1, 0], mate)

    order = [(c, h) for c in range(chunks + 1) for h in range(2)]

    def finish():
        total = fins[...]
        high, low = split(total)
        factors = jnp.concatenate([high, low], axis=0)
        basis = base()
        gw1_ref[...] = contract(jnp.concatenate([basis, basis], axis=0), factors, 0, 0)
        back = contract(factors, w1_ref[...], 1, 1)
        gtp_ref[...] = back[0:rows] + back[rows:]
        grow_ref[...] = total[used : used + 8]

    @pl.when(core != lead)
    def _():
        greet(mate)
        get(5, 6, 0, 1, 2, 3, 4)
        have(5, 6)
        own_cells()
        have(0, 1, 2, 3, 4)
        own_packet()
        pl.semaphore_wait(barrier, half)
        for copy in cell_copies(core, mate):
            copy.start()
        each(1, half, lambda k: packet_copy(k, near(k, lead)).start())
        get(7, 8, 9)
        have(7, 8, 9)
        for copy in cell_copies(core, mate):
            copy.wait_send()
        each(1, half, lambda k: packet_copy(k, near(k, lead)).wait_send())
        for c, h in order:
            give(c, h).wait_recv()
        give_params().wait_recv()
        finish()

    @pl.when(core == lead)
    def _():
        get(0, 1, 2, 3, 4)
        each(0, half, lambda k: greet(far(k, lead)))
        each(1, half, lambda k: greet(near(k, lead)))
        each(0, half, lambda k: greet(near(k, 0)))
        get(5, 6)
        have(0, 1, 2, 3, 4)
        own_packet()
        get(7, 8, 9, 10, 11, 12, 13)
        have(5, 6)
        own_cells()

        def arrival(s):
            return remote(gath.at[s], gath.at[s], g_send.at[0], g_recv.at[s], across)

        def cells_arrive(b):
            for i, part in enumerate((codes_all, pars_all)):
                remote(part.at[b], part.at[b], f_send.at[0, i], f_recv.at[b, i], across).wait_recv()

        def send_first():
            pl.semaphore_wait(barrier, n)
            each(0, half, lambda k: packet_copy(k, far(k, lead)).start())
            for copy in cell_copies(lead, across):
                copy.start()

        def send_second():
            for copy in cell_copies(0, across):
                copy.start()

        @pl.when(upper == 1)
        def _():
            send_first()

        have(7, 8, 9, 10, 11, 12, 13)
        w1t[...] = w1_ref[...].astype(f32).T.astype(bf16)
        w2t[...] = w2_ref[...].astype(f32).T.astype(bf16)
        tpt[...] = base().astype(f32).T.astype(bf16)
        bias[...] = jnp.concatenate(
            [b1_ref[...], b2_ref[...], jnp.zeros((6, hidden), f32)], axis=0
        ).T
        edge = lax.broadcasted_iota(jnp.int32, (ROWS, nf * 2 * cells), 0)
        act1[hidden : hidden + ROWS, :] = jnp.where(edge == 0, 1.0, 0.0).astype(bf16)

        def features(which):
            return jnp.concatenate([feat[block_of(which, c)] for c in range(nf)], axis=1)

        def forward(which):
            here = pl.ds(pl.multiple_of(which * nf * cells, nf * cells), nf * cells)
            hid = contract(tpt[...], features(which), 1, 0).astype(bf16)
            act, slope = silu_parts(contract(w1t[...], hid, 1, 0) + bias[:, 0:1])
            act = act.astype(bf16)
            act1[0:hidden, here] = act
            slope1[:, here] = slope
            act, slope = silu_parts(contract(w2t[...], act, 1, 0) + bias[:, 1:2])
            act2[:, here] = act.astype(bf16)
            slope2[:, here] = slope

        def entries(s, slot):
            column[slot] = gath[s].T
            spot = column[slot, pl.ds(pl.multiple_of(lax.rem(s, per) * local, local), local), :]
            px, py, pz, pf = spot[:, 2:3], spot[:, 3:4], spot[:, 4:5], spot[:, 5:6]
            turn = (wave_low + (wave_high - wave_low) * pf / (freqs - 1)) * (0.5 / math.pi)
            deep = pz * pz
            gain = kernel_gain * pz
            at_re = pl.ds(pl.multiple_of(s * local, local), local)
            at_im = pl.ds(pl.multiple_of(targets + s * local, local), local)
            for b in range(2 * nf):
                chip = place + (b // nf) * half
                first = (chip * nf + b % nf) * cells
                if SIDE % cells == 0:
                    row = (first // SIDE).astype(f32)
                    off = lax.rem(first, SIDE) + lax.broadcasted_iota(jnp.int32, (1, cells), 1)
                    col = off.astype(f32)
                else:
                    index = first + lax.broadcasted_iota(jnp.int32, (1, cells), 1)
                    col = (index % SIDE).astype(f32)
                    row = (index // SIDE).astype(f32)
                off_y = py - row
                off_x = px - col
                square = off_x * off_x + (off_y * off_y + deep)
                inverse = lax.rsqrt(square)
                distance = square * inverse
                phase = distance * turn
                rest = phase - jnp.round(phase)
                power = rest * rest
                sine = rest * horner(power, SINE)
                cosine = horner(power, COSINE)
                amplitude = (inverse * inverse) * gain
                scaled = amplitude * sine
                here = slice(b * cells, (b + 1) * cells)
                waves[at_re, here] = (amplitude - scaled * sine).astype(bf16)
                waves[at_im, here] = (scaled * cosine).astype(bf16)

        def section(first):
            @pl.loop(0, half // 2)
            def _(i):
                pair = (first + 2 * i, first + 2 * i + 1)
                for s in pair:

                    @pl.when(s != me)
                    def _():
                        arrival(s).wait_recv()

                for slot, s in enumerate(pair):
                    entries(s, slot)

        cells_arrive(block_of(upper, 0))

        @pl.when(upper == 1)
        def _():
            send_second()

        for c in range(nf):
            make_features(block_of(upper, c))
        forward(upper)
        section(upper * half)

        @pl.when(upper == 0)
        def _():
            send_first()
            send_second()

        section((1 - upper) * half)

        line = lax.broadcasted_iota(jnp.int32, (outs, width), 0)
        is_re = line < freqs
        freq_line = jnp.where(is_re, line, line - freqs).astype(f32)

        def weigh(group):
            block = gath[group * per]
            for j in range(1, per):
                block = block + gath[group * per + j]
            adj = block[0:2].astype(bf16).astype(f32)
            a0, a1 = adj[0:1], adj[1:2]
            chosen = freq_line == block[5:6]
            to = pl.multiple_of(group * width, width)
            left[:, pl.ds(to, width)] = jnp.where(
                chosen, jnp.where(is_re, a0, a1), 0.0
            ).astype(bf16)
            to = pl.multiple_of(targets + group * width, width)
            left[:, pl.ds(to, width)] = jnp.where(
                chosen, jnp.where(is_re, a1, -a0), 0.0
            ).astype(bf16)

        each(0, n // per, weigh)

        def swap(i, c, h):
            bit = (i + h * (rounds // 2)) % rounds
            side = lax.rem(me // (1 << bit), 2)
            other = me + (1 - 2 * side) * (1 << bit)
            return remote(
                piece(sbuf.at[i], ssml.at[i], c, h),
                piece(rbuf.at[i], rsml.at[i], c, h),
                x_send.at[i, c, h],
                x_recv.at[i, c, h],
                {"cells": other, "freq": lead},
            )

        spec[...] = contract(left[...], waves[...], 1, 0).astype(bf16)
        for c in range(nf):
            cells_arrive(block_of(1 - upper, c))
            make_features(block_of(1 - upper, c))
        forward(1 - upper)
        back = contract(wo_ref[...], spec[...], 1, 0)
        d2[...] = (back * slope2[...]).astype(bf16)

        grad = contract(act1[...], d2[...], 1, 1)
        for c in range(chunks - 1):
            sbuf[0, c] = grad[0:hidden, c * outs : (c + 1) * outs].astype(WIRE)
            for h in range(2):
                swap(0, c, h).start()
        grad_b2 = grad[hidden : hidden + 1]
        sbuf[0, chunks - 1] = contract(act2[...], spec[...], 1, 1).astype(WIRE)
        for h in range(2):
            swap(0, chunks - 1, h).start()

        back = contract(w2_ref[...], d2[...], 1, 0)
        d1[...] = (back * slope1[...]).astype(bf16)
        both = jnp.concatenate([features(which) for which in range(2)], axis=1)
        small = contract(both, d1[...], 1, 1)
        line = lax.broadcasted_iota(jnp.int32, (rows, hidden), 0)
        ssml[0] = jnp.where(line == used + 1, grad_b2, small)
        for h in range(2):
            swap(0, chunks, h).start()

        high, low = split(contract(proj_ref[...], w1_ref[...], 1, 0))
        folded = jnp.concatenate([high.astype(f32), low.astype(f32)], axis=0).astype(bf16)
        own = pl.ds(pl.multiple_of(upper * (nf * cells), nf * cells), nf * cells)
        params = contract(folded, d1[:, own], 1, 0)
        params = params[0:n_par] + params[n_par:]
        gc_mate[...] = params[:, 0:cells]
        gc_ref[...] = params[:, cells:]
        give_params().start()

        for i in range(rounds):
            last = i == rounds - 1
            for c, h in order:
                swap(i, c, h).wait_recv()
                total = (
                    piece(sbuf.at[i], ssml.at[i], c, h)[...].astype(f32)
                    + piece(rbuf.at[i], rsml.at[i], c, h)[...].astype(f32)
                )
                if last:
                    target = piece(fin, fins, c, h)
                    target[...] = (total * scale).astype(target.dtype)
                    give(c, h).start()
                else:
                    target = piece(sbuf.at[i + 1], ssml.at[i + 1], c, h)
                    target[...] = total.astype(target.dtype)
                    swap(i + 1, c, h).start()
        finish()

        each(0, half, lambda k: packet_copy(k, far(k, lead)).wait_send())
        for copy in cell_copies(lead, across) + cell_copies(0, across):
            copy.wait_send()
        for i in range(rounds):
            for c, h in order:
                swap(i, c, h).wait_send()
        for c, h in order:
            give(c, h).wait_send()
        give_params().wait_send()


def unpack(
    fin,
    gc_in,
    gw1_in,
    gtp_in,
    grow_in,
    go_ref,
    gw2_ref,
    gb2_ref,
    gw1_ref,
    gb1_ref,
    gt_ref,
    gp_ref,
    gc_ref,
):
    outs = go_ref.shape[1]
    levels, n_par = gt_ref.shape[0], gp_ref.shape[0]
    last = fin.shape[0] - 1
    go_ref[...] = fin[last].astype(f32)
    for c in range(last):
        gw2_ref[:, c * outs : (c + 1) * outs] = fin[c].astype(f32)
    gw1_ref[...] = gw1_in[...]
    gb1_ref[...] = grow_in[0:1]
    gb2_ref[...] = grow_in[1:2]
    gt_ref[...] = gtp_in[0:levels]
    gp_ref[...] = gtp_in[levels : levels + n_par]
    gc_ref[...] = gc_in[...]


def round_up(value, step):
    return -(-value // step) * step


def body(
    adjoint,
    target_x,
    target_y,
    target_z,
    assignment,
    level_codes,
    cell_params,
    level_table,
    w_proj,
    w_one,
    b_one,
    w_two,
    b_two,
    w_out,
):
    n = lax.axis_size("cells")
    nf = lax.axis_size("freq")
    cells = level_codes.shape[0]
    local = target_x.shape[0]
    hidden = w_one.shape[0]
    levels = level_table.shape[0]
    n_par = w_proj.shape[0]
    outs = w_out.shape[1]
    per = math.gcd(n, max(1, LANES // local))
    half = n // 2
    rounds = half.bit_length() - 1
    assert nf == 2 and n == 2 << rounds
    rows = round_up(levels + n_par + 8, 2 * ROWS)
    chunks = 1 + hidden // outs
    blocks = 2 * nf
    every = blocks * cells
    targets = n * local
    scale = 1.0 / math.sqrt(cells * n * nf)
    vmem = pl.BlockSpec(memory_space=pltpu.VMEM)
    dma = pltpu.SemaphoreType.DMA
    args = (
        adjoint,
        target_x[None, :],
        target_y[None, :],
        target_z[None, :],
        assignment[None, :],
        level_codes[None, :],
        cell_params,
        level_table,
        w_proj,
        w_one,
        b_one[None, :],
        w_two,
        b_two[None, :],
        w_out,
    )
    packed = pl.pallas_call(
        functools.partial(kernel, (n, nf, per, rounds, scale)),
        out_shape=[
            pltpu.VMEM((chunks, hidden, outs), WIRE),
            pltpu.VMEM((rows, hidden), f32),
            pltpu.VMEM((n_par, cells), f32),
            pltpu.VMEM((hidden, hidden), f32),
            pltpu.VMEM((rows, hidden), f32),
            pltpu.VMEM((8, hidden), f32),
        ],
        in_specs=[pl.BlockSpec(memory_space=pltpu.HBM)] * 14,
        out_specs=[vmem] * 6,
        scratch_shapes=[pltpu.VMEM(arg.shape, arg.dtype) for arg in args]
        + [
            pltpu.VMEM((n, 8, per * local), f32),
            pltpu.VMEM((blocks, 1, cells), jnp.int32),
            pltpu.VMEM((blocks, 2 * n_par, cells // 2), bf16),
            pltpu.VMEM((blocks, rows, cells), bf16),
            pltpu.VMEM((2, per * local, 8), f32),
            pltpu.VMEM((hidden, hidden), bf16),
            pltpu.VMEM((hidden, hidden), bf16),
            pltpu.VMEM((hidden, rows), bf16),
            pltpu.VMEM((hidden, 8), f32),
            pltpu.VMEM((hidden + ROWS, every), bf16),
            pltpu.VMEM((hidden, every), f32),
            pltpu.VMEM((hidden, every), bf16),
            pltpu.VMEM((hidden, every), f32),
            pltpu.VMEM((2 * targets, every), bf16),
            pltpu.VMEM((outs, 2 * targets), bf16),
            pltpu.VMEM((outs, every), bf16),
            pltpu.VMEM((hidden, every), bf16),
            pltpu.VMEM((hidden, every), bf16),
            pltpu.VMEM((n_par, cells), f32),
            pltpu.VMEM((rounds, chunks, hidden, outs), WIRE),
            pltpu.VMEM((rounds, rows, hidden), f32),
            pltpu.VMEM((rounds, chunks, hidden, outs), WIRE),
            pltpu.VMEM((rounds, rows, hidden), f32),
            dma((n,)),
            dma((n,)),
            dma((nf, 2)),
            dma((blocks, 2)),
            dma((rounds, chunks + 1, 2)),
            dma((rounds, chunks + 1, 2)),
            dma((chunks + 2, 2)),
            dma((chunks + 2, 2)),
            dma((len(args),)),
        ],
        compiler_params=pltpu.CompilerParams(
            collective_id=0, has_side_effects=True, vmem_limit_bytes=VMEM_GRANT
        ),
        name="hologram_adjoint",
    )(*[pltpu.with_memory_space_constraint(arg, pltpu.HBM) for arg in args])
    fin, _, params, g_one, g_low, g_rows = packed
    results = pl.pallas_call(
        unpack,
        out_shape=[
            jax.ShapeDtypeStruct((hidden, outs), f32),
            jax.ShapeDtypeStruct((hidden, hidden), f32),
            jax.ShapeDtypeStruct((1, hidden), f32),
            jax.ShapeDtypeStruct((hidden, hidden), f32),
            jax.ShapeDtypeStruct((1, hidden), f32),
            jax.ShapeDtypeStruct((levels, hidden), f32),
            jax.ShapeDtypeStruct((n_par, hidden), f32),
            jax.ShapeDtypeStruct((n_par, cells), f32),
        ],
        in_specs=[vmem] * 5,
        out_specs=[vmem] * 8,
        compiler_params=pltpu.CompilerParams(vmem_limit_bytes=VMEM_GRANT // 4),
        name="unpack",
    )(fin, params, g_one, g_low, g_rows)
    grad_out, grad_w2, grad_b2, grad_w1, grad_b1, grad_table, grad_proj, grad_params = results
    return (
        grad_out,
        grad_w2,
        grad_b2[0],
        grad_w1,
        grad_b1[0],
        grad_table,
        grad_proj,
        grad_params,
    )


def solution(mesh):
    split_all = ("groups", "cells", "freq")
    points = ("groups", "cells")
    placed = (
        P(None, points),
        P(points),
        P(points),
        P(points),
        P(points),
        P(split_all),
        P(None, split_all),
    ) + (P(),) * 7
    return jax.shard_map(
        body,
        mesh=mesh,
        in_specs=placed,
        out_specs=(
            P("groups", None),
            P("groups", None),
            P("groups"),
            P("groups", None),
            P("groups"),
            P("groups", None),
            P("groups", None),
            P(None, split_all),
        ),
        check_vma=False,
    )
```

```python
import functools
import math

import jax
import jax.numpy as jnp
from jax import lax
from jax.experimental import pallas as pl
from jax.experimental.pallas import tpu as pltpu
from jax.sharding import PartitionSpec as P

SIDE = 1024
LANES = 128
ROWS = 16
WIRE = jnp.bfloat16
VMEM_GRANT = 50331648

wave_low = 1.0
wave_high = 3.0
kernel_gain = 150.0

SINE = (4.44288292, -7.3082457, 3.60635441, -0.84611289, 0.10982699)
COSINE = (1.4142135, -6.97885099, 5.73946117, -1.88356299, 0.31069819)

f32 = jnp.float32
bf16 = jnp.bfloat16


def contract(left, right, left_dim, right_dim):
    return lax.dot_general(
        left, right, (((left_dim,), (right_dim,)), ((), ())), preferred_element_type=f32
    )


def horner(square, terms):
    total = terms[-1]
    for term in terms[-2::-1]:
        total = total * square + term
    return total


def each(low, high, step):
    if high - low <= 8:
        for k in range(low, high):
            step(k)
    else:

        @pl.loop(low, high)
        def _(k):
            step(k)


def silu_parts(pre):
    sig = 0.5 + 0.5 * jnp.tanh(0.5 * pre)
    act = pre * sig
    return act, sig + act * (1.0 - sig)


def split(value):
    high = value.astype(bf16)
    return high, (value - high.astype(f32)).astype(bf16)


def kernel(dims, *refs):
    inputs, results, loaded = refs[:14], refs[14:20], refs[20:34]
    (
        fin,
        fins,
        gc_ref,
        gw1_ref,
        gtp_ref,
        grow_ref,
    ) = results
    (
        gath,
        codes_all,
        pars_all,
        feat,
        column,
        fold,
        w2t,
        bias,
        act1,
        slope1,
        act2,
        slope2,
        waves,
        left,
        spec,
        d2,
        d1,
        gc_mate,
        sbuf,
        ssml,
        rbuf,
        rsml,
        g_send,
        g_recv,
        f_send,
        f_recv,
        x_send,
        x_recv,
        o_send,
        o_recv,
        load_sem,
    ) = refs[34:]
    (
        adj_ref,
        x_ref,
        y_ref,
        z_ref,
        asg_ref,
        codes_ref,
        params_ref,
        table_ref,
        proj_ref,
        w1_ref,
        b1_ref,
        w2_ref,
        b2_ref,
        wo_ref,
    ) = loaded
    n, nf, per, rounds, scale = dims
    me = lax.axis_index("cells")
    core = lax.axis_index("freq")
    lead = nf - 1
    half = n // 2
    upper = me // half
    place = lax.rem(me, half)
    partner = lax.rem(me + half, n)
    cells = codes_ref.shape[1]
    local = x_ref.shape[1]
    targets = n * local
    hidden = w1_ref.shape[0]
    levels = table_ref.shape[0]
    n_par = proj_ref.shape[0]
    used = levels + n_par
    outs = wo_ref.shape[1]
    freqs = outs // 2
    width = per * local
    rows = feat.shape[1]
    chunks = fin.shape[0]
    batch = column.shape[0]
    top = hidden // 2

    def remote(src, dst, send, recv, device):
        return pltpu.make_async_remote_copy(
            src_ref=src,
            dst_ref=dst,
            send_sem=send,
            recv_sem=recv,
            device_id=device,
            device_id_type=pl.DeviceIdType.MESH,
        )

    def greet(device):
        pl.semaphore_signal(
            barrier, inc=1, device_id=device, device_id_type=pl.DeviceIdType.MESH
        )

    barrier = pltpu.get_barrier_semaphore()
    loads = [
        pltpu.make_async_copy(src, dst, load_sem.at[i])
        for i, (src, dst) in enumerate(zip(inputs, loaded))
    ]

    def get(*which):
        for i in which:
            loads[i].start()

    def have(*which):
        for i in which:
            loads[i].wait()

    def own_cells():
        mine = block_of(upper, core)
        codes_all[mine] = codes_ref[...]
        wide = params_ref[...].astype(f32)
        pars_all[mine] = jnp.concatenate(
            [wide[:, : cells // 2], wide[:, cells // 2 :]], axis=0
        ).astype(bf16)

    def make_features(b):
        level = lax.broadcasted_iota(jnp.int32, (levels, cells), 0)
        line = lax.broadcasted_iota(jnp.int32, (rows - used, cells), 0)
        stacked = pars_all[b].astype(f32)
        feat[b] = jnp.concatenate(
            [
                jnp.where(codes_all[b] == level, 1.0, 0.0),
                jnp.concatenate([stacked[0:n_par], stacked[n_par:]], axis=1),
                jnp.where(line == 0, 1.0, 0.0),
            ],
            axis=0,
        ).astype(bf16)

    def base():
        return jnp.concatenate(
            [
                table_ref[...].astype(f32),
                proj_ref[...].astype(f32),
                jnp.zeros((rows - used, hidden), f32),
            ],
            axis=0,
        ).astype(bf16)

    def block_of(which, c):
        return which * nf + c

    mate = {"freq": nf - 1 - core}
    across = {"cells": partner, "freq": lead}

    def cell_copies(c, device):
        mine = block_of(upper, c)
        return [
            remote(part.at[mine], part.at[mine], f_send.at[c, i], f_recv.at[mine, i], device)
            for i, part in enumerate((codes_all, pars_all))
        ]

    def near(k, c):
        return {"cells": upper * half + lax.rem(place + k, half), "freq": c}

    def far(k, c):
        return {"cells": (1 - upper) * half + lax.rem(place + k, half), "freq": c}

    def packet_copy(k, device):
        return remote(gath.at[me], gath.at[me], g_send.at[k], g_recv.at[me], device)

    def own_packet():
        packet = jnp.concatenate(
            [
                adj_ref[...],
                x_ref[...],
                y_ref[...],
                z_ref[...],
                asg_ref[...].astype(f32),
                jnp.zeros((2, local), f32),
            ],
            axis=0,
        )
        spread = jnp.concatenate([packet] * per, axis=1)
        lane = lax.broadcasted_iota(jnp.int32, (8, width), 1)
        start = lax.rem(me, per) * local
        inside = jnp.logical_and(lane >= start, lane < start + local)
        gath[me] = jnp.where(inside, spread, 0.0)

    def rows_of(h):
        return pl.ds(h * top, top)

    def small_of(h):
        return pl.ds(h * (rows // 2), rows // 2)

    def piece(buffer, small, c, h):
        if c < chunks:
            return buffer.at[c, rows_of(h)]
        return small.at[small_of(h)]

    def give(c, h):
        view = piece(fin, fins, c, h)
        return remote(view, view, o_send.at[c, h], o_recv.at[c, h], mate)

    def give_params():
        return remote(gc_mate, gc_ref, o_send.at[chunks + 1, 0], o_recv.at[chunks + 1, 0], mate)

    order = [(c, h) for c in range(chunks + 1) for h in range(2)]

    def finish():
        total = fins[...]
        high, low = split(total)
        factors = jnp.concatenate([high, low], axis=0)
        basis = base()
        gw1_ref[...] = contract(jnp.concatenate([basis, basis], axis=0), factors, 0, 0)
        back = contract(factors, w1_ref[...], 1, 1)
        gtp_ref[...] = back[0:rows] + back[rows:]
        grow_ref[...] = total[used : used + 8]

    @pl.when(core != lead)
    def _():
        greet(mate)
        get(5, 6, 0, 1, 2, 3, 4)
        have(5, 6)
        own_cells()
        have(0, 1, 2, 3, 4)
        own_packet()
        pl.semaphore_wait(barrier, half)
        for copy in cell_copies(core, mate):
            copy.start()
        each(1, half, lambda k: packet_copy(k, near(k, lead)).start())
        get(7, 8, 9)
        have(7, 8, 9)
        for copy in cell_copies(core, mate):
            copy.wait_send()
        each(1, half, lambda k: packet_copy(k, near(k, lead)).wait_send())
        for c, h in order:
            give(c, h).wait_recv()
        give_params().wait_recv()
        finish()

    @pl.when(core == lead)
    def _():
        get(0, 1, 2, 3, 4, 5, 6)
        each(0, half, lambda k: greet(far(k, lead)))
        each(1, half, lambda k: greet(near(k, lead)))
        each(0, half, lambda k: greet(near(k, 0)))
        have(0, 1, 2, 3, 4)
        own_packet()

        def arrival(s):
            return remote(gath.at[s], gath.at[s], g_send.at[0], g_recv.at[s], across)

        def cells_arrive(b):
            for i, part in enumerate((codes_all, pars_all)):
                remote(part.at[b], part.at[b], f_send.at[0, i], f_recv.at[b, i], across).wait_recv()

        def send_packets():
            pl.semaphore_wait(barrier, n)
            each(0, half, lambda k: packet_copy(k, far(k, lead)).start())

        def send_cells(c):
            for copy in cell_copies(c, across):
                copy.start()

        @pl.when(upper == 1)
        def _():
            send_packets()

        get(7, 8, 9, 10, 11, 12, 13)
        have(5, 6)
        own_cells()

        @pl.when(upper == 1)
        def _():
            send_cells(lead)

        have(7, 8, 9, 10, 11, 12, 13)
        folded = contract(base(), w1_ref[...], 1, 0)
        line = lax.broadcasted_iota(jnp.int32, (rows, hidden), 0)
        folded = jnp.where(line == used, b1_ref[...], folded)
        high = folded.astype(bf16).astype(f32)
        fold[...] = jnp.concatenate([high, folded - high], axis=0).T.astype(bf16)
        w2t[...] = w2_ref[...].astype(f32).T.astype(bf16)
        bias[...] = jnp.concatenate(
            [b2_ref[...], jnp.zeros((7, hidden), f32)], axis=0
        ).T
        edge = lax.broadcasted_iota(jnp.int32, (ROWS, nf * 2 * cells), 0)
        act1[hidden : hidden + ROWS, :] = jnp.where(edge == 0, 1.0, 0.0).astype(bf16)

        def features(which):
            return jnp.concatenate([feat[block_of(which, c)] for c in range(nf)], axis=1)

        def forward(which):
            here = pl.ds(pl.multiple_of(which * nf * cells, nf * cells), nf * cells)
            known = features(which)
            act, slope = silu_parts(
                contract(fold[...], jnp.concatenate([known, known], axis=0), 1, 0)
            )
            act = act.astype(bf16)
            act1[0:hidden, here] = act
            slope1[:, here] = slope
            act, slope = silu_parts(contract(w2t[...], act, 1, 0) + bias[:, 0:1])
            act2[:, here] = act.astype(bf16)
            slope2[:, here] = slope

        def entries(s, slot):
            spot = column[slot, pl.ds(pl.multiple_of(lax.rem(s, per) * local, local), local), :]
            px, py, pz, pf = spot[:, 2:3], spot[:, 3:4], spot[:, 4:5], spot[:, 5:6]
            turn = (wave_low + (wave_high - wave_low) * pf / (freqs - 1)) * (0.5 / math.pi)
            deep = pz * pz
            gain = kernel_gain * pz
            at_re = pl.ds(pl.multiple_of(s * local, local), local)
            at_im = pl.ds(pl.multiple_of(targets + s * local, local), local)
            for b in range(2 * nf):
                chip = place + (b // nf) * half
                first = (chip * nf + b % nf) * cells
                if SIDE % cells == 0:
                    row = (first // SIDE).astype(f32)
                    off = lax.rem(first, SIDE) + lax.broadcasted_iota(jnp.int32, (1, cells), 1)
                    col = off.astype(f32)
                else:
                    index = first + lax.broadcasted_iota(jnp.int32, (1, cells), 1)
                    col = (index % SIDE).astype(f32)
                    row = (index // SIDE).astype(f32)
                off_y = py - row
                off_x = px - col
                square = off_x * off_x + (off_y * off_y + deep)
                inverse = lax.rsqrt(square)
                distance = square * inverse
                phase = distance * turn
                rest = phase - jnp.round(phase)
                power = rest * rest
                sine = rest * horner(power, SINE)
                cosine = horner(power, COSINE)
                amplitude = (inverse * inverse) * gain
                scaled = amplitude * sine
                here = slice(b * cells, (b + 1) * cells)
                waves[at_re, here] = (amplitude - scaled * sine).astype(bf16)
                waves[at_im, here] = (scaled * cosine).astype(bf16)

        def section(first):
            @pl.loop(0, half // batch)
            def _(i):
                sources = [first + batch * i + j for j in range(batch)]
                for s in sources:

                    @pl.when(s != me)
                    def _():
                        arrival(s).wait_recv()

                for slot, s in enumerate(sources):
                    column[slot] = gath[s].T
                for slot, s in enumerate(sources):
                    entries(s, slot)

        cells_arrive(block_of(upper, 0))

        @pl.when(upper == 1)
        def _():
            send_cells(0)

        for c in range(nf):
            make_features(block_of(upper, c))
        forward(upper)

        @pl.when(upper == 0)
        def _():
            send_packets()
            send_cells(lead)
            send_cells(0)

        section(upper * half)
        section((1 - upper) * half)

        line = lax.broadcasted_iota(jnp.int32, (outs, width), 0)
        is_re = line < freqs
        freq_line = jnp.where(is_re, line, line - freqs).astype(f32)

        def weigh(group):
            block = gath[group * per]
            for j in range(1, per):
                block = block + gath[group * per + j]
            adj = block[0:2].astype(bf16).astype(f32)
            a0, a1 = adj[0:1], adj[1:2]
            chosen = freq_line == block[5:6]
            to = pl.multiple_of(group * width, width)
            left[:, pl.ds(to, width)] = jnp.where(
                chosen, jnp.where(is_re, a0, a1), 0.0
            ).astype(bf16)
            to = pl.multiple_of(targets + group * width, width)
            left[:, pl.ds(to, width)] = jnp.where(
                chosen, jnp.where(is_re, a1, -a0), 0.0
            ).astype(bf16)

        each(0, n // per, weigh)

        def swap(i, c, h):
            bit = (i + h * (rounds // 2)) % rounds
            side = lax.rem(me // (1 << bit), 2)
            other = me + (1 - 2 * side) * (1 << bit)
            return remote(
                piece(sbuf.at[i], ssml.at[i], c, h),
                piece(rbuf.at[i], rsml.at[i], c, h),
                x_send.at[i, c, h],
                x_recv.at[i, c, h],
                {"cells": other, "freq": lead},
            )

        spec[...] = contract(left[...], waves[...], 1, 0).astype(bf16)
        for c in range(nf):
            cells_arrive(block_of(1 - upper, c))
            make_features(block_of(1 - upper, c))
        forward(1 - upper)
        back = contract(wo_ref[...], spec[...], 1, 0)
        d2[...] = (back * slope2[...]).astype(bf16)

        grad = contract(act1[...], d2[...], 1, 1)
        for c in range(chunks - 1):
            sbuf[0, c] = grad[0:hidden, c * outs : (c + 1) * outs].astype(WIRE)
            for h in range(2):
                swap(0, c, h).start()
        grad_b2 = grad[hidden : hidden + 1]
        sbuf[0, chunks - 1] = contract(act2[...], spec[...], 1, 1).astype(WIRE)
        for h in range(2):
            swap(0, chunks - 1, h).start()

        back = contract(w2_ref[...], d2[...], 1, 0)
        d1[...] = (back * slope1[...]).astype(bf16)
        both = jnp.concatenate([features(which) for which in range(2)], axis=1)
        small = contract(both, d1[...], 1, 1)
        line = lax.broadcasted_iota(jnp.int32, (rows, hidden), 0)
        ssml[0] = jnp.where(line == used + 1, grad_b2, small)
        for h in range(2):
            swap(0, chunks, h).start()

        high, low = split(contract(proj_ref[...], w1_ref[...], 1, 0))
        folded = jnp.concatenate([high.astype(f32), low.astype(f32)], axis=0).astype(bf16)
        own = pl.ds(pl.multiple_of(upper * (nf * cells), nf * cells), nf * cells)
        params = contract(folded, d1[:, own], 1, 0)
        params = params[0:n_par] + params[n_par:]
        gc_mate[...] = params[:, 0:cells]
        gc_ref[...] = params[:, cells:]
        give_params().start()

        for i in range(rounds):
            last = i == rounds - 1
            for c, h in order:
                swap(i, c, h).wait_recv()
                total = (
                    piece(sbuf.at[i], ssml.at[i], c, h)[...].astype(f32)
                    + piece(rbuf.at[i], rsml.at[i], c, h)[...].astype(f32)
                )
                if last:
                    target = piece(fin, fins, c, h)
                    target[...] = (total * scale).astype(target.dtype)
                    give(c, h).start()
                else:
                    target = piece(sbuf.at[i + 1], ssml.at[i + 1], c, h)
                    target[...] = total.astype(target.dtype)
                    swap(i + 1, c, h).start()
        finish()

        each(0, half, lambda k: packet_copy(k, far(k, lead)).wait_send())
        for copy in cell_copies(lead, across) + cell_copies(0, across):
            copy.wait_send()
        for i in range(rounds):
            for c, h in order:
                swap(i, c, h).wait_send()
        for c, h in order:
            give(c, h).wait_send()
        give_params().wait_send()


def unpack(
    fin,
    gc_in,
    gw1_in,
    gtp_in,
    grow_in,
    go_ref,
    gw2_ref,
    gb2_ref,
    gw1_ref,
    gb1_ref,
    gt_ref,
    gp_ref,
    gc_ref,
):
    outs = go_ref.shape[1]
    levels, n_par = gt_ref.shape[0], gp_ref.shape[0]
    last = fin.shape[0] - 1
    go_ref[...] = fin[last].astype(f32)
    for c in range(last):
        gw2_ref[:, c * outs : (c + 1) * outs] = fin[c].astype(f32)
    gw1_ref[...] = gw1_in[...]
    gb1_ref[...] = grow_in[0:1]
    gb2_ref[...] = grow_in[1:2]
    gt_ref[...] = gtp_in[0:levels]
    gp_ref[...] = gtp_in[levels : levels + n_par]
    gc_ref[...] = gc_in[...]


def round_up(value, step):
    return -(-value // step) * step


def body(
    adjoint,
    target_x,
    target_y,
    target_z,
    assignment,
    level_codes,
    cell_params,
    level_table,
    w_proj,
    w_one,
    b_one,
    w_two,
    b_two,
    w_out,
):
    n = lax.axis_size("cells")
    nf = lax.axis_size("freq")
    cells = level_codes.shape[0]
    local = target_x.shape[0]
    hidden = w_one.shape[0]
    levels = level_table.shape[0]
    n_par = w_proj.shape[0]
    outs = w_out.shape[1]
    per = math.gcd(n, max(1, LANES // local))
    half = n // 2
    rounds = half.bit_length() - 1
    assert nf == 2 and n == 2 << rounds
    rows = round_up(levels + n_par + 8, 2 * ROWS)
    chunks = 1 + hidden // outs
    blocks = 2 * nf
    every = blocks * cells
    targets = n * local
    scale = 1.0 / math.sqrt(cells * n * nf)
    vmem = pl.BlockSpec(memory_space=pltpu.VMEM)
    dma = pltpu.SemaphoreType.DMA
    args = (
        adjoint,
        target_x[None, :],
        target_y[None, :],
        target_z[None, :],
        assignment[None, :],
        level_codes[None, :],
        cell_params,
        level_table,
        w_proj,
        w_one,
        b_one[None, :],
        w_two,
        b_two[None, :],
        w_out,
    )
    packed = pl.pallas_call(
        functools.partial(kernel, (n, nf, per, rounds, scale)),
        out_shape=[
            pltpu.VMEM((chunks, hidden, outs), WIRE),
            pltpu.VMEM((rows, hidden), f32),
            pltpu.VMEM((n_par, cells), f32),
            pltpu.VMEM((hidden, hidden), f32),
            pltpu.VMEM((rows, hidden), f32),
            pltpu.VMEM((8, hidden), f32),
        ],
        in_specs=[pl.BlockSpec(memory_space=pltpu.HBM)] * 14,
        out_specs=[vmem] * 6,
        scratch_shapes=[pltpu.VMEM(arg.shape, arg.dtype) for arg in args]
        + [
            pltpu.VMEM((n, 8, per * local), f32),
            pltpu.VMEM((blocks, 1, cells), jnp.int32),
            pltpu.VMEM((blocks, 2 * n_par, cells // 2), bf16),
            pltpu.VMEM((blocks, rows, cells), bf16),
            pltpu.VMEM((min(half, 4), per * local, 8), f32),
            pltpu.VMEM((hidden, 2 * rows), bf16),
            pltpu.VMEM((hidden, hidden), bf16),
            pltpu.VMEM((hidden, 8), f32),
            pltpu.VMEM((hidden + ROWS, every), bf16),
            pltpu.VMEM((hidden, every), f32),
            pltpu.VMEM((hidden, every), bf16),
            pltpu.VMEM((hidden, every), f32),
            pltpu.VMEM((2 * targets, every), bf16),
            pltpu.VMEM((outs, 2 * targets), bf16),
            pltpu.VMEM((outs, every), bf16),
            pltpu.VMEM((hidden, every), bf16),
            pltpu.VMEM((hidden, every), bf16),
            pltpu.VMEM((n_par, cells), f32),
            pltpu.VMEM((rounds, chunks, hidden, outs), WIRE),
            pltpu.VMEM((rounds, rows, hidden), f32),
            pltpu.VMEM((rounds, chunks, hidden, outs), WIRE),
            pltpu.VMEM((rounds, rows, hidden), f32),
            dma((n,)),
            dma((n,)),
            dma((nf, 2)),
            dma((blocks, 2)),
            dma((rounds, chunks + 1, 2)),
            dma((rounds, chunks + 1, 2)),
            dma((chunks + 2, 2)),
            dma((chunks + 2, 2)),
            dma((len(args),)),
        ],
        compiler_params=pltpu.CompilerParams(
            collective_id=0, has_side_effects=True, vmem_limit_bytes=VMEM_GRANT
        ),
        name="hologram_adjoint",
    )(*[pltpu.with_memory_space_constraint(arg, pltpu.HBM) for arg in args])
    fin, _, params, g_one, g_low, g_rows = packed
    results = pl.pallas_call(
        unpack,
        out_shape=[
            jax.ShapeDtypeStruct((hidden, outs), f32),
            jax.ShapeDtypeStruct((hidden, hidden), f32),
            jax.ShapeDtypeStruct((1, hidden), f32),
            jax.ShapeDtypeStruct((hidden, hidden), f32),
            jax.ShapeDtypeStruct((1, hidden), f32),
            jax.ShapeDtypeStruct((levels, hidden), f32),
            jax.ShapeDtypeStruct((n_par, hidden), f32),
            jax.ShapeDtypeStruct((n_par, cells), f32),
        ],
        in_specs=[vmem] * 5,
        out_specs=[vmem] * 8,
        compiler_params=pltpu.CompilerParams(vmem_limit_bytes=VMEM_GRANT // 4),
        name="unpack",
    )(fin, params, g_one, g_low, g_rows)
    grad_out, grad_w2, grad_b2, grad_w1, grad_b1, grad_table, grad_proj, grad_params = results
    return (
        grad_out,
        grad_w2,
        grad_b2[0],
        grad_w1,
        grad_b1[0],
        grad_table,
        grad_proj,
        grad_params,
    )


def solution(mesh):
    split_all = ("groups", "cells", "freq")
    points = ("groups", "cells")
    placed = (
        P(None, points),
        P(points),
        P(points),
        P(points),
        P(points),
        P(split_all),
        P(None, split_all),
    ) + (P(),) * 7
    return jax.shard_map(
        body,
        mesh=mesh,
        in_specs=placed,
        out_specs=(
            P("groups", None),
            P("groups", None),
            P("groups"),
            P("groups", None),
            P("groups"),
            P("groups", None),
            P("groups", None),
            P(None, split_all),
        ),
        check_vma=False,
    )
```

```python
import functools
import math

import jax
import jax.numpy as jnp
from jax import lax
from jax.experimental import pallas as pl
from jax.experimental.pallas import tpu as pltpu
from jax.sharding import PartitionSpec as P

SIDE = 1024
LANES = 128
ROWS = 16
WIRE = jnp.bfloat16
VMEM_GRANT = 50331648

wave_low = 1.0
wave_high = 3.0
kernel_gain = 150.0

SINE = (4.44288292, -7.3082457, 3.60635441, -0.84611289, 0.10982699)
COSINE = (1.4142135, -6.97885099, 5.73946117, -1.88356299, 0.31069819)

f32 = jnp.float32
bf16 = jnp.bfloat16


def contract(left, right, left_dim, right_dim):
    return lax.dot_general(
        left, right, (((left_dim,), (right_dim,)), ((), ())), preferred_element_type=f32
    )


def horner(square, terms):
    total = terms[-1]
    for term in terms[-2::-1]:
        total = total * square + term
    return total


def each(low, high, step):
    if high - low <= 8:
        for k in range(low, high):
            step(k)
    else:

        @pl.loop(low, high)
        def _(k):
            step(k)


def silu_parts(pre):
    sig = 0.5 + 0.5 * jnp.tanh(0.5 * pre)
    act = pre * sig
    return act, sig + act * (1.0 - sig)


def split(value):
    high = value.astype(bf16)
    return high, (value - high.astype(f32)).astype(bf16)


def kernel(dims, *refs):
    inputs, results, loaded = refs[:14], refs[14:20], refs[20:34]
    (
        fin,
        fins,
        gc_ref,
        gw1_ref,
        gtp_ref,
        grow_ref,
    ) = results
    (
        gath,
        codes_all,
        pars_all,
        feat,
        column,
        fold,
        w2t,
        bias,
        act1,
        slope1,
        act2,
        slope2,
        waves,
        left,
        spec,
        d2,
        d1,
        gc_mate,
        sbuf,
        rbuf,
        rsml,
        g_send,
        g_recv,
        f_send,
        f_recv,
        x_send,
        x_recv,
        s_send,
        s_recv,
        o_send,
        o_recv,
        load_sem,
    ) = refs[34:]
    (
        adj_ref,
        x_ref,
        y_ref,
        z_ref,
        asg_ref,
        codes_ref,
        params_ref,
        table_ref,
        proj_ref,
        w1_ref,
        b1_ref,
        w2_ref,
        b2_ref,
        wo_ref,
    ) = loaded
    n, nf, per, rounds, scale = dims
    me = lax.axis_index("cells")
    core = lax.axis_index("freq")
    lead = nf - 1
    half = n // 2
    upper = me // half
    place = lax.rem(me, half)
    partner = lax.rem(me + half, n)
    cells = codes_ref.shape[1]
    local = x_ref.shape[1]
    targets = n * local
    hidden = w1_ref.shape[0]
    levels = table_ref.shape[0]
    n_par = proj_ref.shape[0]
    used = levels + n_par
    outs = wo_ref.shape[1]
    freqs = outs // 2
    width = per * local
    rows = feat.shape[1]
    chunks = fin.shape[0]
    batch = column.shape[0]
    top = hidden // 2

    def remote(src, dst, send, recv, device):
        return pltpu.make_async_remote_copy(
            src_ref=src,
            dst_ref=dst,
            send_sem=send,
            recv_sem=recv,
            device_id=device,
            device_id_type=pl.DeviceIdType.MESH,
        )

    def greet(device):
        pl.semaphore_signal(
            barrier, inc=1, device_id=device, device_id_type=pl.DeviceIdType.MESH
        )

    barrier = pltpu.get_barrier_semaphore()
    loads = [
        pltpu.make_async_copy(src, dst, load_sem.at[i])
        for i, (src, dst) in enumerate(zip(inputs, loaded))
    ]

    def get(*which):
        for i in which:
            loads[i].start()

    def have(*which):
        for i in which:
            loads[i].wait()

    def own_cells():
        mine = block_of(upper, core)
        codes_all[mine] = codes_ref[...]
        wide = params_ref[...].astype(f32)
        pars_all[mine] = jnp.concatenate(
            [wide[:, : cells // 2], wide[:, cells // 2 :]], axis=0
        ).astype(bf16)

    def make_features(b):
        level = lax.broadcasted_iota(jnp.int32, (levels, cells), 0)
        line = lax.broadcasted_iota(jnp.int32, (rows - used, cells), 0)
        stacked = pars_all[b].astype(f32)
        feat[b] = jnp.concatenate(
            [
                jnp.where(codes_all[b] == level, 1.0, 0.0),
                jnp.concatenate([stacked[0:n_par], stacked[n_par:]], axis=1),
                jnp.where(line == 0, 1.0, 0.0),
            ],
            axis=0,
        ).astype(bf16)

    def base():
        return jnp.concatenate(
            [
                table_ref[...].astype(f32),
                proj_ref[...].astype(f32),
                jnp.zeros((rows - used, hidden), f32),
            ],
            axis=0,
        ).astype(bf16)

    def block_of(which, c):
        return which * nf + c

    mate = {"freq": nf - 1 - core}
    across = {"cells": partner, "freq": lead}

    def cell_copies(c, device, slot=None):
        slot = c if slot is None else slot
        mine = block_of(upper, c)
        return [
            remote(part.at[mine], part.at[mine], f_send.at[slot, i], f_recv.at[mine, i], device)
            for i, part in enumerate((codes_all, pars_all))
        ]

    def near(k, c):
        return {"cells": upper * half + lax.rem(place + k, half), "freq": c}

    def far(k, c):
        return {"cells": (1 - upper) * half + lax.rem(place + k, half), "freq": c}

    def packet_copy(k, device):
        return remote(gath.at[me], gath.at[me], g_send.at[k], g_recv.at[me], device)

    def own_packet():
        packet = jnp.concatenate(
            [
                adj_ref[...],
                x_ref[...],
                y_ref[...],
                z_ref[...],
                asg_ref[...].astype(f32),
                jnp.zeros((2, local), f32),
            ],
            axis=0,
        )
        spread = jnp.concatenate([packet] * per, axis=1)
        lane = lax.broadcasted_iota(jnp.int32, (8, width), 1)
        start = lax.rem(me, per) * local
        inside = jnp.logical_and(lane >= start, lane < start + local)
        gath[me] = jnp.where(inside, spread, 0.0)

    def rows_of(h):
        return pl.ds(h * top, top)

    def piece(buffer, c, h):
        return buffer.at[c, rows_of(h)]

    def give(c, h):
        view = piece(fin, c, h)
        return remote(view, view, o_send.at[c, h], o_recv.at[c, h], mate)

    def give_small():
        return remote(fins, fins, o_send.at[chunks, 0], o_recv.at[chunks, 0], mate)

    def give_params():
        return remote(gc_mate, gc_ref, o_send.at[chunks + 1, 0], o_recv.at[chunks + 1, 0], mate)

    order = [(c, h) for c in range(chunks) for h in range(2)]

    def finish():
        total = fins[...]
        high, low = split(total)
        factors = jnp.concatenate([high, low], axis=0)
        basis = base()
        gw1_ref[...] = contract(jnp.concatenate([basis, basis], axis=0), factors, 0, 0)
        back = contract(factors, w1_ref[...], 1, 1)
        gtp_ref[...] = back[0:rows] + back[rows:]
        grow_ref[...] = total[used : used + 8]

    @pl.when(core != lead)
    def _():
        greet(mate)
        get(5, 6, 0, 1, 2, 3, 4)
        have(5, 6)
        own_cells()
        have(0, 1, 2, 3, 4)
        own_packet()

        @pl.when(upper == 0)
        def _():
            pl.semaphore_wait(barrier, half)

        @pl.when(upper == 1)
        def _():
            pl.semaphore_wait(barrier, half + 1)
            for copy in cell_copies(core, across, nf):
                copy.start()

        for copy in cell_copies(core, mate):
            copy.start()
        each(1, half, lambda k: packet_copy(k, near(k, lead)).start())
        get(7, 8, 9)
        have(7, 8, 9)
        for copy in cell_copies(core, mate):
            copy.wait_send()

        @pl.when(upper == 1)
        def _():
            for copy in cell_copies(core, across, nf):
                copy.wait_send()

        each(1, half, lambda k: packet_copy(k, near(k, lead)).wait_send())
        give_params().wait_recv()
        give_small().wait_recv()
        finish()
        for c, h in order:
            give(c, h).wait_recv()

    @pl.when(core == lead)
    def _():
        get(0, 1, 2, 3, 4, 5, 6)
        each(0, half, lambda k: greet(far(k, lead)))
        each(1, half, lambda k: greet(near(k, lead)))
        each(0, half, lambda k: greet(near(k, 0)))

        @pl.when(upper == 0)
        def _():
            greet(far(0, 0))

        have(0, 1, 2, 3, 4)
        own_packet()

        def arrival(s):
            return remote(gath.at[s], gath.at[s], g_send.at[0], g_recv.at[s], across)

        def cells_arrive(b):
            for i, part in enumerate((codes_all, pars_all)):
                remote(part.at[b], part.at[b], f_send.at[0, i], f_recv.at[b, i], across).wait_recv()

        def send_packets():
            pl.semaphore_wait(barrier, n)
            each(0, half, lambda k: packet_copy(k, far(k, lead)).start())

        def send_cells(c):
            for copy in cell_copies(c, across):
                copy.start()

        @pl.when(upper == 1)
        def _():
            send_packets()

        get(7, 8, 9, 10, 11, 12, 13)
        have(5, 6)
        own_cells()

        @pl.when(upper == 1)
        def _():
            send_cells(lead)

        have(7, 8, 9, 10, 11, 12, 13)
        folded = contract(base(), w1_ref[...], 1, 0)
        line = lax.broadcasted_iota(jnp.int32, (rows, hidden), 0)
        folded = jnp.where(line == used, b1_ref[...], folded)
        high = folded.astype(bf16).astype(f32)
        fold[...] = jnp.concatenate([high, folded - high], axis=0).T.astype(bf16)
        w2t[...] = w2_ref[...].astype(f32).T.astype(bf16)
        bias[...] = jnp.concatenate(
            [b2_ref[...], jnp.zeros((7, hidden), f32)], axis=0
        ).T
        edge = lax.broadcasted_iota(jnp.int32, (ROWS, nf * 2 * cells), 0)
        act1[hidden : hidden + ROWS, :] = jnp.where(edge == 0, 1.0, 0.0).astype(bf16)

        def features(which):
            return jnp.concatenate([feat[block_of(which, c)] for c in range(nf)], axis=1)

        def forward(which):
            here = pl.ds(pl.multiple_of(which * nf * cells, nf * cells), nf * cells)
            known = features(which)
            act, slope = silu_parts(
                contract(fold[...], jnp.concatenate([known, known], axis=0), 1, 0)
            )
            act = act.astype(bf16)
            act1[0:hidden, here] = act
            slope1[:, here] = slope
            act, slope = silu_parts(contract(w2t[...], act, 1, 0) + bias[:, 0:1])
            act2[:, here] = act.astype(bf16)
            slope2[:, here] = slope

        def entries(s, slot):
            spot = column[slot, pl.ds(pl.multiple_of(lax.rem(s, per) * local, local), local), :]
            px, py, pz, pf = spot[:, 2:3], spot[:, 3:4], spot[:, 4:5], spot[:, 5:6]
            turn = (wave_low + (wave_high - wave_low) * pf / (freqs - 1)) * (0.5 / math.pi)
            deep = pz * pz
            gain = kernel_gain * pz
            at_re = pl.ds(pl.multiple_of(s * local, local), local)
            at_im = pl.ds(pl.multiple_of(targets + s * local, local), local)
            for b in range(2 * nf):
                chip = place + (b // nf) * half
                first = (chip * nf + b % nf) * cells
                if SIDE % cells == 0:
                    row = (first // SIDE).astype(f32)
                    off = lax.rem(first, SIDE) + lax.broadcasted_iota(jnp.int32, (1, cells), 1)
                    col = off.astype(f32)
                else:
                    index = first + lax.broadcasted_iota(jnp.int32, (1, cells), 1)
                    col = (index % SIDE).astype(f32)
                    row = (index // SIDE).astype(f32)
                off_y = py - row
                off_x = px - col
                square = off_x * off_x + (off_y * off_y + deep)
                inverse = lax.rsqrt(square)
                distance = square * inverse
                phase = distance * turn
                rest = phase - jnp.round(phase)
                power = rest * rest
                sine = rest * horner(power, SINE)
                cosine = horner(power, COSINE)
                amplitude = (inverse * inverse) * gain
                scaled = amplitude * sine
                here = slice(b * cells, (b + 1) * cells)
                waves[at_re, here] = (amplitude - scaled * sine).astype(bf16)
                waves[at_im, here] = (scaled * cosine).astype(bf16)

        def section(first):
            @pl.loop(0, half // batch)
            def _(i):
                sources = [first + batch * i + j for j in range(batch)]
                for s in sources:

                    @pl.when(s != me)
                    def _():
                        arrival(s).wait_recv()

                for slot, s in enumerate(sources):
                    column[slot] = gath[s].T
                for slot, s in enumerate(sources):
                    entries(s, slot)

        cells_arrive(block_of(upper, 0))

        for c in range(nf):
            make_features(block_of(upper, c))
        forward(upper)

        @pl.when(upper == 0)
        def _():
            send_packets()
            send_cells(lead)
            send_cells(0)

        section(upper * half)
        for c in range(nf):
            cells_arrive(block_of(1 - upper, c))
            make_features(block_of(1 - upper, c))
        forward(1 - upper)
        section((1 - upper) * half)

        line = lax.broadcasted_iota(jnp.int32, (outs, width), 0)
        is_re = line < freqs
        freq_line = jnp.where(is_re, line, line - freqs).astype(f32)

        def weigh(group):
            block = gath[group * per]
            for j in range(1, per):
                block = block + gath[group * per + j]
            adj = block[0:2].astype(bf16).astype(f32)
            a0, a1 = adj[0:1], adj[1:2]
            chosen = freq_line == block[5:6]
            to = pl.multiple_of(group * width, width)
            left[:, pl.ds(to, width)] = jnp.where(
                chosen, jnp.where(is_re, a0, a1), 0.0
            ).astype(bf16)
            to = pl.multiple_of(targets + group * width, width)
            left[:, pl.ds(to, width)] = jnp.where(
                chosen, jnp.where(is_re, a1, -a0), 0.0
            ).astype(bf16)

        each(0, n // per, weigh)

        def swap(i, c, h):
            bit = (i + h * (rounds // 2)) % rounds
            side = lax.rem(me // (1 << bit), 2)
            other = me + (1 - 2 * side) * (1 << bit)
            return remote(
                piece(sbuf.at[i], c, h),
                piece(rbuf.at[i], c, h),
                x_send.at[i, c, h],
                x_recv.at[i, c, h],
                {"cells": other, "freq": lead},
            )

        spec[...] = contract(left[...], waves[...], 1, 0).astype(bf16)
        sbuf[0, 0] = contract(act2[...], spec[...], 1, 1).astype(WIRE)
        for h in range(2):
            swap(0, 0, h).start()
        back = contract(wo_ref[...], spec[...], 1, 0)
        d2[...] = (back * slope2[...]).astype(bf16)

        grad = contract(act1[...], d2[...], 1, 1)
        for c in range(1, chunks):
            sbuf[0, c] = grad[0:hidden, (c - 1) * outs : c * outs].astype(WIRE)
            for h in range(2):
                swap(0, c, h).start()
        grad_b2 = grad[hidden : hidden + 1]

        back = contract(w2_ref[...], d2[...], 1, 0)
        d1[...] = (back * slope1[...]).astype(bf16)
        both = jnp.concatenate([features(which) for which in range(2)], axis=1)
        small = contract(both, d1[...], 1, 1)
        line = lax.broadcasted_iota(jnp.int32, (rows, hidden), 0)
        rsml[place] = jnp.where(line == used + 1, grad_b2, small)

        def small_copy(k):
            mine = rsml.at[place]
            return remote(mine, mine, s_send.at[k], s_recv.at[place], near(k, lead))

        def small_arrival(k):
            spot = lax.rem(place + k, half)
            held = rsml.at[spot]
            return remote(held, held, s_send.at[0], s_recv.at[spot], across)

        each(1, half, lambda k: small_copy(k).start())

        high, low = split(contract(proj_ref[...], w1_ref[...], 1, 0))
        folded = jnp.concatenate([high.astype(f32), low.astype(f32)], axis=0).astype(bf16)
        own = pl.ds(pl.multiple_of(upper * (nf * cells), nf * cells), nf * cells)
        params = contract(folded, d1[:, own], 1, 0)
        params = params[0:n_par] + params[n_par:]
        gc_mate[...] = params[:, 0:cells]
        gc_ref[...] = params[:, cells:]
        give_params().start()

        for i in range(rounds):
            last = i == rounds - 1
            for c, h in order:
                if last and (c, h) == order[-2]:
                    each(1, half, lambda k: small_arrival(k).wait_recv())
                    total = rsml[0]
                    if half <= 8:
                        for k in range(1, half):
                            total = total + rsml[k]
                    else:
                        total = lax.fori_loop(1, half, lambda k, acc: acc + rsml[k], total)
                    fins[...] = total * scale
                    give_small().start()
                swap(i, c, h).wait_recv()
                total = (
                    piece(sbuf.at[i], c, h)[...].astype(f32)
                    + piece(rbuf.at[i], c, h)[...].astype(f32)
                )
                if last:
                    piece(fin, c, h)[...] = (total * scale).astype(WIRE)
                    give(c, h).start()
                else:
                    piece(sbuf.at[i + 1], c, h)[...] = total.astype(WIRE)
                    swap(i + 1, c, h).start()
        finish()

        each(1, half, lambda k: small_copy(k).wait_send())
        give_small().wait_send()
        each(0, half, lambda k: packet_copy(k, far(k, lead)).wait_send())
        for copy in cell_copies(lead, across):
            copy.wait_send()

        @pl.when(upper == 0)
        def _():
            for copy in cell_copies(0, across):
                copy.wait_send()

        for i in range(rounds):
            for c, h in order:
                swap(i, c, h).wait_send()
        for c, h in order:
            give(c, h).wait_send()
        give_params().wait_send()


def unpack(
    fin,
    gc_in,
    gw1_in,
    gtp_in,
    grow_in,
    go_ref,
    gw2_ref,
    gb2_ref,
    gw1_ref,
    gb1_ref,
    gt_ref,
    gp_ref,
    gc_ref,
):
    outs = go_ref.shape[1]
    levels, n_par = gt_ref.shape[0], gp_ref.shape[0]
    go_ref[...] = fin[0].astype(f32)
    for c in range(1, fin.shape[0]):
        gw2_ref[:, (c - 1) * outs : c * outs] = fin[c].astype(f32)
    gw1_ref[...] = gw1_in[...]
    gb1_ref[...] = grow_in[0:1]
    gb2_ref[...] = grow_in[1:2]
    gt_ref[...] = gtp_in[0:levels]
    gp_ref[...] = gtp_in[levels : levels + n_par]
    gc_ref[...] = gc_in[...]


def round_up(value, step):
    return -(-value // step) * step


def body(
    adjoint,
    target_x,
    target_y,
    target_z,
    assignment,
    level_codes,
    cell_params,
    level_table,
    w_proj,
    w_one,
    b_one,
    w_two,
    b_two,
    w_out,
):
    n = lax.axis_size("cells")
    nf = lax.axis_size("freq")
    cells = level_codes.shape[0]
    local = target_x.shape[0]
    hidden = w_one.shape[0]
    levels = level_table.shape[0]
    n_par = w_proj.shape[0]
    outs = w_out.shape[1]
    per = math.gcd(n, max(1, LANES // local))
    half = n // 2
    rounds = half.bit_length() - 1
    assert nf == 2 and n == 2 << rounds
    rows = round_up(levels + n_par + 8, 2 * ROWS)
    chunks = 1 + hidden // outs
    blocks = 2 * nf
    every = blocks * cells
    targets = n * local
    scale = 1.0 / math.sqrt(cells * n * nf)
    vmem = pl.BlockSpec(memory_space=pltpu.VMEM)
    dma = pltpu.SemaphoreType.DMA
    args = (
        adjoint,
        target_x[None, :],
        target_y[None, :],
        target_z[None, :],
        assignment[None, :],
        level_codes[None, :],
        cell_params,
        level_table,
        w_proj,
        w_one,
        b_one[None, :],
        w_two,
        b_two[None, :],
        w_out,
    )
    packed = pl.pallas_call(
        functools.partial(kernel, (n, nf, per, rounds, scale)),
        out_shape=[
            pltpu.VMEM((chunks, hidden, outs), WIRE),
            pltpu.VMEM((rows, hidden), f32),
            pltpu.VMEM((n_par, cells), f32),
            pltpu.VMEM((hidden, hidden), f32),
            pltpu.VMEM((rows, hidden), f32),
            pltpu.VMEM((8, hidden), f32),
        ],
        in_specs=[pl.BlockSpec(memory_space=pltpu.HBM)] * 14,
        out_specs=[vmem] * 6,
        scratch_shapes=[pltpu.VMEM(arg.shape, arg.dtype) for arg in args]
        + [
            pltpu.VMEM((n, 8, per * local), f32),
            pltpu.VMEM((blocks, 1, cells), jnp.int32),
            pltpu.VMEM((blocks, 2 * n_par, cells // 2), bf16),
            pltpu.VMEM((blocks, rows, cells), bf16),
            pltpu.VMEM((min(half, 4), per * local, 8), f32),
            pltpu.VMEM((hidden, 2 * rows), bf16),
            pltpu.VMEM((hidden, hidden), bf16),
            pltpu.VMEM((hidden, 8), f32),
            pltpu.VMEM((hidden + ROWS, every), bf16),
            pltpu.VMEM((hidden, every), f32),
            pltpu.VMEM((hidden, every), bf16),
            pltpu.VMEM((hidden, every), f32),
            pltpu.VMEM((2 * targets, every), bf16),
            pltpu.VMEM((outs, 2 * targets), bf16),
            pltpu.VMEM((outs, every), bf16),
            pltpu.VMEM((hidden, every), bf16),
            pltpu.VMEM((hidden, every), bf16),
            pltpu.VMEM((n_par, cells), f32),
            pltpu.VMEM((rounds, chunks, hidden, outs), WIRE),
            pltpu.VMEM((rounds, chunks, hidden, outs), WIRE),
            pltpu.VMEM((half, rows, hidden), f32),
            dma((n,)),
            dma((n,)),
            dma((nf + 1, 2)),
            dma((blocks, 2)),
            dma((rounds, chunks, 2)),
            dma((rounds, chunks, 2)),
            dma((half,)),
            dma((half,)),
            dma((chunks + 2, 2)),
            dma((chunks + 2, 2)),
            dma((len(args),)),
        ],
        compiler_params=pltpu.CompilerParams(
            collective_id=0, has_side_effects=True, vmem_limit_bytes=VMEM_GRANT
        ),
        name="hologram_adjoint",
    )(*[pltpu.with_memory_space_constraint(arg, pltpu.HBM) for arg in args])
    fin, _, params, g_one, g_low, g_rows = packed
    results = pl.pallas_call(
        unpack,
        out_shape=[
            jax.ShapeDtypeStruct((hidden, outs), f32),
            jax.ShapeDtypeStruct((hidden, hidden), f32),
            jax.ShapeDtypeStruct((1, hidden), f32),
            jax.ShapeDtypeStruct((hidden, hidden), f32),
            jax.ShapeDtypeStruct((1, hidden), f32),
            jax.ShapeDtypeStruct((levels, hidden), f32),
            jax.ShapeDtypeStruct((n_par, hidden), f32),
            jax.ShapeDtypeStruct((n_par, cells), f32),
        ],
        in_specs=[vmem] * 5,
        out_specs=[vmem] * 8,
        compiler_params=pltpu.CompilerParams(vmem_limit_bytes=VMEM_GRANT // 4),
        name="unpack",
    )(fin, params, g_one, g_low, g_rows)
    grad_out, grad_w2, grad_b2, grad_w1, grad_b1, grad_table, grad_proj, grad_params = results
    return (
        grad_out,
        grad_w2,
        grad_b2[0],
        grad_w1,
        grad_b1[0],
        grad_table,
        grad_proj,
        grad_params,
    )


def solution(mesh):
    split_all = ("groups", "cells", "freq")
    points = ("groups", "cells")
    placed = (
        P(None, points),
        P(points),
        P(points),
        P(points),
        P(points),
        P(split_all),
        P(None, split_all),
    ) + (P(),) * 7
    return jax.shard_map(
        body,
        mesh=mesh,
        in_specs=placed,
        out_specs=(
            P("groups", None),
            P("groups", None),
            P("groups"),
            P("groups", None),
            P("groups"),
            P("groups", None),
            P("groups", None),
            P(None, split_all),
        ),
        check_vma=False,
    )
```

```python
import functools
import math

import jax
import jax.numpy as jnp
from jax import lax
from jax.experimental import pallas as pl
from jax.experimental.pallas import tpu as pltpu
from jax.sharding import PartitionSpec as P

SIDE = 1024
LANES = 128
ROWS = 16
WIRE = jnp.bfloat16
VMEM_GRANT = 50331648

wave_low = 1.0
wave_high = 3.0
kernel_gain = 150.0

SINE = (4.44288292, -7.3082457, 3.60635441, -0.84611289, 0.10982699)
COSINE = (1.4142135, -6.97885099, 5.73946117, -1.88356299, 0.31069819)

f32 = jnp.float32
bf16 = jnp.bfloat16


def contract(left, right, left_dim, right_dim):
    return lax.dot_general(
        left, right, (((left_dim,), (right_dim,)), ((), ())), preferred_element_type=f32
    )


def horner(square, terms):
    total = terms[-1]
    for term in terms[-2::-1]:
        total = total * square + term
    return total


def each(low, high, step):
    if high - low <= 8:
        for k in range(low, high):
            step(k)
    else:

        @pl.loop(low, high)
        def _(k):
            step(k)


def silu_parts(pre):
    sig = 0.5 + 0.5 * jnp.tanh(0.5 * pre)
    act = pre * sig
    return act, sig + act * (1.0 - sig)


def split(value):
    high = value.astype(bf16)
    return high, (value - high.astype(f32)).astype(bf16)


def kernel(dims, *refs):
    inputs, results, loaded = refs[:14], refs[14:20], refs[20:34]
    (
        fin,
        fins,
        gc_ref,
        gw1_ref,
        gtp_ref,
        grow_ref,
    ) = results
    (
        gath,
        codes_all,
        pars_all,
        feat,
        column,
        fold,
        w2t,
        bias,
        act1,
        slope1,
        act2,
        slope2,
        waves,
        left,
        spec,
        d2,
        d1,
        gc_mate,
        sbuf,
        rbuf,
        rsml,
        g_send,
        g_recv,
        f_send,
        f_recv,
        x_send,
        x_recv,
        s_send,
        s_recv,
        o_send,
        o_recv,
        load_sem,
    ) = refs[34:]
    (
        adj_ref,
        x_ref,
        y_ref,
        z_ref,
        asg_ref,
        codes_ref,
        params_ref,
        table_ref,
        proj_ref,
        w1_ref,
        b1_ref,
        w2_ref,
        b2_ref,
        wo_ref,
    ) = loaded
    n, nf, per, rounds, scale = dims
    me = lax.axis_index("cells")
    core = lax.axis_index("freq")
    lead = nf - 1
    half = n // 2
    upper = me // half
    place = lax.rem(me, half)
    partner = lax.rem(me + half, n)
    cells = codes_ref.shape[1]
    local = x_ref.shape[1]
    targets = n * local
    hidden = w1_ref.shape[0]
    levels = table_ref.shape[0]
    n_par = proj_ref.shape[0]
    used = levels + n_par
    outs = wo_ref.shape[1]
    freqs = outs // 2
    width = per * local
    rows = feat.shape[1]
    chunks = fin.shape[0]
    batch = column.shape[0]
    top = hidden // 2

    def remote(src, dst, send, recv, device):
        return pltpu.make_async_remote_copy(
            src_ref=src,
            dst_ref=dst,
            send_sem=send,
            recv_sem=recv,
            device_id=device,
            device_id_type=pl.DeviceIdType.MESH,
        )

    def greet(device):
        pl.semaphore_signal(
            barrier, inc=1, device_id=device, device_id_type=pl.DeviceIdType.MESH
        )

    barrier = pltpu.get_barrier_semaphore()
    loads = [
        pltpu.make_async_copy(src, dst, load_sem.at[i])
        for i, (src, dst) in enumerate(zip(inputs, loaded))
    ]

    def get(*which):
        for i in which:
            loads[i].start()

    def have(*which):
        for i in which:
            loads[i].wait()

    def own_cells():
        mine = block_of(upper, core)
        codes_all[mine] = codes_ref[...]
        wide = params_ref[...].astype(f32)
        pars_all[mine] = jnp.concatenate(
            [wide[:, : cells // 2], wide[:, cells // 2 :]], axis=0
        ).astype(bf16)

    def make_features(b):
        level = lax.broadcasted_iota(jnp.int32, (levels, cells), 0)
        line = lax.broadcasted_iota(jnp.int32, (rows - used, cells), 0)
        stacked = pars_all[b].astype(f32)
        feat[b] = jnp.concatenate(
            [
                jnp.where(codes_all[b] == level, 1.0, 0.0),
                jnp.concatenate([stacked[0:n_par], stacked[n_par:]], axis=1),
                jnp.where(line == 0, 1.0, 0.0),
            ],
            axis=0,
        ).astype(bf16)

    def base():
        return jnp.concatenate(
            [
                table_ref[...].astype(f32),
                proj_ref[...].astype(f32),
                jnp.zeros((rows - used, hidden), f32),
            ],
            axis=0,
        ).astype(bf16)

    def block_of(which, c):
        return which * nf + c

    mate = {"freq": nf - 1 - core}
    across = {"cells": partner, "freq": lead}

    def cell_copies(c, device, slot=None):
        slot = c if slot is None else slot
        mine = block_of(upper, c)
        return [
            remote(part.at[mine], part.at[mine], f_send.at[slot, i], f_recv.at[mine, i], device)
            for i, part in enumerate((codes_all, pars_all))
        ]

    def near(k, c):
        return {"cells": upper * half + lax.rem(place + k, half), "freq": c}

    def far(k, c):
        return {"cells": (1 - upper) * half + lax.rem(place + k, half), "freq": c}

    def packet_copy(k, device):
        return remote(gath.at[me], gath.at[me], g_send.at[k], g_recv.at[me], device)

    def own_packet():
        packet = jnp.concatenate(
            [
                adj_ref[...],
                x_ref[...],
                y_ref[...],
                z_ref[...],
                asg_ref[...].astype(f32),
                jnp.zeros((2, local), f32),
            ],
            axis=0,
        )
        spread = jnp.concatenate([packet] * per, axis=1)
        lane = lax.broadcasted_iota(jnp.int32, (8, width), 1)
        start = lax.rem(me, per) * local
        inside = jnp.logical_and(lane >= start, lane < start + local)
        gath[me] = jnp.where(inside, spread, 0.0)

    def rows_of(h):
        return pl.ds(h * top, top)

    def piece(buffer, c, h):
        return buffer.at[c, rows_of(h)]

    def give(c, h):
        view = piece(fin, c, h)
        return remote(view, view, o_send.at[c, h], o_recv.at[c, h], mate)

    def give_small():
        return remote(fins, fins, o_send.at[chunks, 0], o_recv.at[chunks, 0], mate)

    def give_params():
        return remote(gc_mate, gc_ref, o_send.at[chunks + 1, 0], o_recv.at[chunks + 1, 0], mate)

    order = [(c, h) for c in range(chunks) for h in range(2)]

    def finish():
        total = fins[...]
        high, low = split(total)
        factors = jnp.concatenate([high, low], axis=0)
        basis = base()
        gw1_ref[...] = contract(jnp.concatenate([basis, basis], axis=0), factors, 0, 0)
        back = contract(factors, w1_ref[...], 1, 1)
        gtp_ref[...] = back[0:rows] + back[rows:]
        grow_ref[...] = total[used : used + 8]

    @pl.when(core != lead)
    def _():
        greet(mate)
        get(5, 6, 0, 1, 2, 3, 4)
        have(5, 6)
        own_cells()
        have(0, 1, 2, 3, 4)
        own_packet()

        @pl.when(upper == 0)
        def _():
            pl.semaphore_wait(barrier, half)

        @pl.when(upper == 1)
        def _():
            pl.semaphore_wait(barrier, half + 1)
            for copy in cell_copies(core, across, nf):
                copy.start()

        for copy in cell_copies(core, mate):
            copy.start()
        each(1, half, lambda k: packet_copy(k, near(k, lead)).start())
        get(7, 8, 9)
        have(7, 8, 9)
        for copy in cell_copies(core, mate):
            copy.wait_send()

        @pl.when(upper == 1)
        def _():
            for copy in cell_copies(core, across, nf):
                copy.wait_send()

        each(1, half, lambda k: packet_copy(k, near(k, lead)).wait_send())
        give_params().wait_recv()
        give_small().wait_recv()
        finish()
        for c, h in order:
            give(c, h).wait_recv()

    @pl.when(core == lead)
    def _():
        get(0, 1, 2, 3, 4, 5, 6)
        each(0, half, lambda k: greet(far(k, lead)))
        each(1, half, lambda k: greet(near(k, lead)))
        each(0, half, lambda k: greet(near(k, 0)))

        @pl.when(upper == 0)
        def _():
            greet(far(0, 0))

        have(0, 1, 2, 3, 4)
        own_packet()

        def arrival(s):
            return remote(gath.at[s], gath.at[s], g_send.at[0], g_recv.at[s], across)

        def cells_arrive(b):
            for i, part in enumerate((codes_all, pars_all)):
                remote(part.at[b], part.at[b], f_send.at[0, i], f_recv.at[b, i], across).wait_recv()

        def send_packets():
            pl.semaphore_wait(barrier, n)
            each(0, half, lambda k: packet_copy(k, far(k, lead)).start())

        def send_cells(c):
            for copy in cell_copies(c, across):
                copy.start()

        @pl.when(upper == 1)
        def _():
            send_packets()

        get(7, 8, 9, 10, 11, 12, 13)
        have(5, 6)
        own_cells()

        @pl.when(upper == 1)
        def _():
            send_cells(lead)

        have(7, 8, 9, 10, 11, 12, 13)
        folded = contract(base(), w1_ref[...], 1, 0)
        line = lax.broadcasted_iota(jnp.int32, (rows, hidden), 0)
        folded = jnp.where(line == used, b1_ref[...], folded)
        high = folded.astype(bf16).astype(f32)
        fold[...] = jnp.concatenate([high, folded - high], axis=0).T.astype(bf16)
        w2t[...] = w2_ref[...].astype(f32).T.astype(bf16)
        bias[...] = jnp.concatenate(
            [b2_ref[...], jnp.zeros((7, hidden), f32)], axis=0
        ).T
        edge = lax.broadcasted_iota(jnp.int32, (ROWS, nf * 2 * cells), 0)
        act1[hidden : hidden + ROWS, :] = jnp.where(edge == 0, 1.0, 0.0).astype(bf16)

        def features(which):
            return jnp.concatenate([feat[block_of(which, c)] for c in range(nf)], axis=1)

        def forward(which):
            here = pl.ds(pl.multiple_of(which * nf * cells, nf * cells), nf * cells)
            known = features(which)
            act, slope = silu_parts(
                contract(fold[...], jnp.concatenate([known, known], axis=0), 1, 0)
            )
            act = act.astype(bf16)
            act1[0:hidden, here] = act
            slope1[:, here] = slope
            act, slope = silu_parts(contract(w2t[...], act, 1, 0) + bias[:, 0:1])
            act2[:, here] = act.astype(bf16)
            slope2[:, here] = slope

        def entries(s, slot):
            spot = column[slot, pl.ds(pl.multiple_of(lax.rem(s, per) * local, local), local), :]
            px, py, pz, pf = spot[:, 2:3], spot[:, 3:4], spot[:, 4:5], spot[:, 5:6]
            turn = (wave_low + (wave_high - wave_low) * pf / (freqs - 1)) * (0.5 / math.pi)
            deep = pz * pz
            gain = kernel_gain * pz
            at_re = pl.ds(pl.multiple_of(s * local, local), local)
            at_im = pl.ds(pl.multiple_of(targets + s * local, local), local)
            for b in range(2 * nf):
                chip = place + (b // nf) * half
                first = (chip * nf + b % nf) * cells
                if SIDE % cells == 0:
                    row = (first // SIDE).astype(f32)
                    off = lax.rem(first, SIDE) + lax.broadcasted_iota(jnp.int32, (1, cells), 1)
                    col = off.astype(f32)
                else:
                    index = first + lax.broadcasted_iota(jnp.int32, (1, cells), 1)
                    col = (index % SIDE).astype(f32)
                    row = (index // SIDE).astype(f32)
                off_y = py - row
                off_x = px - col
                square = off_x * off_x + (off_y * off_y + deep)
                inverse = lax.rsqrt(square)
                distance = square * inverse
                phase = distance * turn
                rest = phase - jnp.round(phase)
                power = rest * rest
                sine = rest * horner(power, SINE)
                cosine = horner(power, COSINE)
                amplitude = (inverse * inverse) * gain
                scaled = amplitude * sine
                here = slice(b * cells, (b + 1) * cells)
                waves[at_re, here] = (amplitude - scaled * sine).astype(bf16)
                waves[at_im, here] = (scaled * cosine).astype(bf16)

        def section(first):
            @pl.loop(0, half // batch)
            def _(i):
                sources = [first + batch * i + j for j in range(batch)]
                for s in sources:

                    @pl.when(s != me)
                    def _():
                        arrival(s).wait_recv()

                for slot, s in enumerate(sources):
                    column[slot] = gath[s].T
                for slot, s in enumerate(sources):
                    entries(s, slot)

        cells_arrive(block_of(upper, 0))

        for c in range(nf):
            make_features(block_of(upper, c))
        forward(upper)

        @pl.when(upper == 0)
        def _():
            send_packets()
            send_cells(lead)
            send_cells(0)

        section(upper * half)
        for c in range(nf):
            cells_arrive(block_of(1 - upper, c))
            make_features(block_of(1 - upper, c))
        forward(1 - upper)
        section((1 - upper) * half)

        line = lax.broadcasted_iota(jnp.int32, (outs, width), 0)
        is_re = line < freqs
        freq_line = jnp.where(is_re, line, line - freqs).astype(f32)

        def weigh(group):
            block = gath[group * per]
            for j in range(1, per):
                block = block + gath[group * per + j]
            adj = block[0:2].astype(bf16).astype(f32)
            a0, a1 = adj[0:1], adj[1:2]
            chosen = freq_line == block[5:6]
            to = pl.multiple_of(group * width, width)
            left[:, pl.ds(to, width)] = jnp.where(
                chosen, jnp.where(is_re, a0, a1), 0.0
            ).astype(bf16)
            to = pl.multiple_of(targets + group * width, width)
            left[:, pl.ds(to, width)] = jnp.where(
                chosen, jnp.where(is_re, a1, -a0), 0.0
            ).astype(bf16)

        each(0, n // per, weigh)

        def swap(i, c, h):
            bit = (i + h * (rounds // 2)) % rounds
            side = lax.rem(me // (1 << bit), 2)
            other = me + (1 - 2 * side) * (1 << bit)
            return remote(
                piece(sbuf.at[i], c, h),
                piece(rbuf.at[i], c, h),
                x_send.at[i, c, h],
                x_recv.at[i, c, h],
                {"cells": other, "freq": lead},
            )

        spec[...] = contract(left[...], waves[...], 1, 0).astype(bf16)
        sbuf[0, 0] = contract(act2[...], spec[...], 1, 1).astype(WIRE)
        for h in range(2):
            swap(0, 0, h).start()
        back = contract(wo_ref[...], spec[...], 1, 0)
        d2[...] = (back * slope2[...]).astype(bf16)

        grad = contract(act1[...], d2[...], 1, 1)
        for c in range(1, chunks):
            sbuf[0, c] = grad[0:hidden, (c - 1) * outs : c * outs].astype(WIRE)
            for h in range(2):
                swap(0, c, h).start()
        grad_b2 = grad[hidden : hidden + 1]

        back = contract(w2_ref[...], d2[...], 1, 0)
        d1[...] = (back * slope1[...]).astype(bf16)
        both = jnp.concatenate([features(which) for which in range(2)], axis=1)
        small = contract(both, d1[...], 1, 1)
        line = lax.broadcasted_iota(jnp.int32, (rows, hidden), 0)
        rsml[place] = jnp.where(line == used + 1, grad_b2, small)

        def small_copy(k):
            mine = rsml.at[place]
            return remote(mine, mine, s_send.at[k], s_recv.at[place], near(k, lead))

        def small_arrival(k):
            spot = lax.rem(place + k, half)
            held = rsml.at[spot]
            return remote(held, held, s_send.at[0], s_recv.at[spot], across)

        each(1, half, lambda k: small_copy(k).start())

        high, low = split(contract(proj_ref[...], w1_ref[...], 1, 0))
        folded = jnp.concatenate([high.astype(f32), low.astype(f32)], axis=0).astype(bf16)
        own = pl.ds(pl.multiple_of(upper * (nf * cells), nf * cells), nf * cells)
        params = contract(folded, d1[:, own], 1, 0)
        params = params[0:n_par] + params[n_par:]
        gc_mate[...] = params[:, 0:cells]
        gc_ref[...] = params[:, cells:]
        give_params().start()

        for i in range(rounds):
            last = i == rounds - 1
            for c, h in order:
                if last and (c, h) == order[-1]:
                    each(1, half, lambda k: small_arrival(k).wait_recv())
                    total = rsml[0]
                    if half <= 8:
                        for k in range(1, half):
                            total = total + rsml[k]
                    else:
                        total = lax.fori_loop(1, half, lambda k, acc: acc + rsml[k], total)
                    fins[...] = total * scale
                    give_small().start()
                swap(i, c, h).wait_recv()
                total = (
                    piece(sbuf.at[i], c, h)[...].astype(f32)
                    + piece(rbuf.at[i], c, h)[...].astype(f32)
                )
                if last:
                    piece(fin, c, h)[...] = (total * scale).astype(WIRE)
                    give(c, h).start()
                else:
                    piece(sbuf.at[i + 1], c, h)[...] = total.astype(WIRE)
                    swap(i + 1, c, h).start()
        finish()

        each(1, half, lambda k: small_copy(k).wait_send())
        give_small().wait_send()
        each(0, half, lambda k: packet_copy(k, far(k, lead)).wait_send())
        for copy in cell_copies(lead, across):
            copy.wait_send()

        @pl.when(upper == 0)
        def _():
            for copy in cell_copies(0, across):
                copy.wait_send()

        for i in range(rounds):
            for c, h in order:
                swap(i, c, h).wait_send()
        for c, h in order:
            give(c, h).wait_send()
        give_params().wait_send()


def unpack(
    fin,
    gc_in,
    gw1_in,
    gtp_in,
    grow_in,
    go_ref,
    gw2_ref,
    gb2_ref,
    gw1_ref,
    gb1_ref,
    gt_ref,
    gp_ref,
    gc_ref,
):
    outs = go_ref.shape[1]
    levels, n_par = gt_ref.shape[0], gp_ref.shape[0]
    go_ref[...] = fin[0].astype(f32)
    for c in range(1, fin.shape[0]):
        gw2_ref[:, (c - 1) * outs : c * outs] = fin[c].astype(f32)
    gw1_ref[...] = gw1_in[...]
    gb1_ref[...] = grow_in[0:1]
    gb2_ref[...] = grow_in[1:2]
    gt_ref[...] = gtp_in[0:levels]
    gp_ref[...] = gtp_in[levels : levels + n_par]
    gc_ref[...] = gc_in[...]


def round_up(value, step):
    return -(-value // step) * step


def body(
    adjoint,
    target_x,
    target_y,
    target_z,
    assignment,
    level_codes,
    cell_params,
    level_table,
    w_proj,
    w_one,
    b_one,
    w_two,
    b_two,
    w_out,
):
    n = lax.axis_size("cells")
    nf = lax.axis_size("freq")
    cells = level_codes.shape[0]
    local = target_x.shape[0]
    hidden = w_one.shape[0]
    levels = level_table.shape[0]
    n_par = w_proj.shape[0]
    outs = w_out.shape[1]
    per = math.gcd(n, max(1, LANES // local))
    half = n // 2
    rounds = half.bit_length() - 1
    assert nf == 2 and n == 2 << rounds
    rows = round_up(levels + n_par + 8, 2 * ROWS)
    chunks = 1 + hidden // outs
    blocks = 2 * nf
    every = blocks * cells
    targets = n * local
    scale = 1.0 / math.sqrt(cells * n * nf)
    vmem = pl.BlockSpec(memory_space=pltpu.VMEM)
    dma = pltpu.SemaphoreType.DMA
    args = (
        adjoint,
        target_x[None, :],
        target_y[None, :],
        target_z[None, :],
        assignment[None, :],
        level_codes[None, :],
        cell_params,
        level_table,
        w_proj,
        w_one,
        b_one[None, :],
        w_two,
        b_two[None, :],
        w_out,
    )
    packed = pl.pallas_call(
        functools.partial(kernel, (n, nf, per, rounds, scale)),
        out_shape=[
            pltpu.VMEM((chunks, hidden, outs), WIRE),
            pltpu.VMEM((rows, hidden), f32),
            pltpu.VMEM((n_par, cells), f32),
            pltpu.VMEM((hidden, hidden), f32),
            pltpu.VMEM((rows, hidden), f32),
            pltpu.VMEM((8, hidden), f32),
        ],
        in_specs=[pl.BlockSpec(memory_space=pltpu.HBM)] * 14,
        out_specs=[vmem] * 6,
        scratch_shapes=[pltpu.VMEM(arg.shape, arg.dtype) for arg in args]
        + [
            pltpu.VMEM((n, 8, per * local), f32),
            pltpu.VMEM((blocks, 1, cells), jnp.int32),
            pltpu.VMEM((blocks, 2 * n_par, cells // 2), bf16),
            pltpu.VMEM((blocks, rows, cells), bf16),
            pltpu.VMEM((min(half, 4), per * local, 8), f32),
            pltpu.VMEM((hidden, 2 * rows), bf16),
            pltpu.VMEM((hidden, hidden), bf16),
            pltpu.VMEM((hidden, 8), f32),
            pltpu.VMEM((hidden + ROWS, every), bf16),
            pltpu.VMEM((hidden, every), f32),
            pltpu.VMEM((hidden, every), bf16),
            pltpu.VMEM((hidden, every), f32),
            pltpu.VMEM((2 * targets, every), bf16),
            pltpu.VMEM((outs, 2 * targets), bf16),
            pltpu.VMEM((outs, every), bf16),
            pltpu.VMEM((hidden, every), bf16),
            pltpu.VMEM((hidden, every), bf16),
            pltpu.VMEM((n_par, cells), f32),
            pltpu.VMEM((rounds, chunks, hidden, outs), WIRE),
            pltpu.VMEM((rounds, chunks, hidden, outs), WIRE),
            pltpu.VMEM((half, rows, hidden), f32),
            dma((n,)),
            dma((n,)),
            dma((nf + 1, 2)),
            dma((blocks, 2)),
            dma((rounds, chunks, 2)),
            dma((rounds, chunks, 2)),
            dma((half,)),
            dma((half,)),
            dma((chunks + 2, 2)),
            dma((chunks + 2, 2)),
            dma((len(args),)),
        ],
        compiler_params=pltpu.CompilerParams(
            collective_id=0, has_side_effects=True, vmem_limit_bytes=VMEM_GRANT
        ),
        name="hologram_adjoint",
    )(*[pltpu.with_memory_space_constraint(arg, pltpu.HBM) for arg in args])
    fin, _, params, g_one, g_low, g_rows = packed
    results = pl.pallas_call(
        unpack,
        out_shape=[
            jax.ShapeDtypeStruct((hidden, outs), f32),
            jax.ShapeDtypeStruct((hidden, hidden), f32),
            jax.ShapeDtypeStruct((1, hidden), f32),
            jax.ShapeDtypeStruct((hidden, hidden), f32),
            jax.ShapeDtypeStruct((1, hidden), f32),
            jax.ShapeDtypeStruct((levels, hidden), f32),
            jax.ShapeDtypeStruct((n_par, hidden), f32),
            jax.ShapeDtypeStruct((n_par, cells), f32),
        ],
        in_specs=[vmem] * 5,
        out_specs=[vmem] * 8,
        compiler_params=pltpu.CompilerParams(vmem_limit_bytes=VMEM_GRANT // 4),
        name="unpack",
    )(fin, params, g_one, g_low, g_rows)
    grad_out, grad_w2, grad_b2, grad_w1, grad_b1, grad_table, grad_proj, grad_params = results
    return (
        grad_out,
        grad_w2,
        grad_b2[0],
        grad_w1,
        grad_b1[0],
        grad_table,
        grad_proj,
        grad_params,
    )


def solution(mesh):
    split_all = ("groups", "cells", "freq")
    points = ("groups", "cells")
    placed = (
        P(None, points),
        P(points),
        P(points),
        P(points),
        P(points),
        P(split_all),
        P(None, split_all),
    ) + (P(),) * 7
    return jax.shard_map(
        body,
        mesh=mesh,
        in_specs=placed,
        out_specs=(
            P("groups", None),
            P("groups", None),
            P("groups"),
            P("groups", None),
            P("groups"),
            P("groups", None),
            P("groups", None),
            P(None, split_all),
        ),
        check_vma=False,
    )
```
